256 devices in a mesh: dom: 64 (over x, z, core), blk: 4 (over y).
Axes of the slice: x: 4, y: 4, z: 8, core: 2. Of those that a mesh axis runs over, the one named last changes fastest.
Arguments:
- hessian: float32 [256, 15, 192, 192], P('dom')
- neighbours: int32 [256, 15], P('dom'), may hold values from 0 to 255, as said below
- counts: int32 [256], P('dom'), may hold values from 5 to 15
- basis_vectors: float32 [512, 49152], P('blk', 'dom')
Outputs:
- blocks: float32 [2, 64, 49152], P(None, 'blk', 'dom')
- factors: float32 [2, 64, 64], replicated
The draws below stay inside these ranges and needn't reach their ends.
Inputs may be any that keep to these rules, and one draw needn't show every extreme that they name: `neighbours`: entry 0 of tile t's list is t itself; the others are distinct tiles of the domains within two of t's domain, cyclically, where tile t belongs to domain t // 4.
All inputs are finite; a program needn't handle non-finite values.
Results may differ from the reference program's by a relative error of at most 0.00024.
Values sent between devices are 32-bit elements; how exact they have to be, the bound alone decides.
No kernel may reach another device: no remote copies, remote signals or barrier semaphores. Data moves between devices by JAX's collectives and lax.ppermute only.
A program may use at most 64 MiB of HBM per device.

```python
import math
import jax
import jax.numpy as jnp
from jax import lax

TILE_ROWS = 192
NEIGHBOURS = 15
BLOCK = 64
STORED = 512
TILES_DEV = 4
N_DOM = 64


def draw_hessian(key, part):
    key_noise, key_diag = jax.random.split(jax.random.fold_in(key, 11))
    full_shape = (TILES_DEV * N_DOM, NEIGHBOURS, TILE_ROWS, TILE_ROWS)
    random_part = jax.random.normal(key_noise, full_shape, jnp.float32)
    random_part = random_part * (NEIGHBOURS * TILE_ROWS) ** (-0.5)
    diag_scale = jnp.exp(jax.random.uniform(key_diag, (TILES_DEV * N_DOM, TILE_ROWS), jnp.float32, 0.0, math.log(4.0)))
    identity = (jnp.arange(TILE_ROWS)[:, None] == jnp.arange(TILE_ROWS)[None, :]).astype(jnp.float32)
    self_block = (jnp.arange(NEIGHBOURS) == 0).astype(jnp.float32)
    return random_part + self_block[None, :, None, None] * diag_scale[:, None, :, None] * identity[None, None, :, :]


def draw_neighbours(key, part):
    tile_total = TILES_DEV * N_DOM
    span = 5 * TILES_DEV
    tile_keys = jax.random.split(jax.random.fold_in(key, 3), tile_total)

    def one_tile(tile_key, tile_id):
        shuffled = jax.random.permutation(tile_key, span - 1)[:NEIGHBOURS - 1]
        own_slot = 2 * TILES_DEV + tile_id % TILES_DEV
        position = jnp.where(shuffled >= own_slot, shuffled + 1, shuffled)
        domain = (tile_id // TILES_DEV + position // TILES_DEV - 2) % N_DOM
        others = domain * TILES_DEV + position % TILES_DEV
        return jnp.concatenate([tile_id[None], others]).astype(jnp.int32)
    return jax.vmap(one_tile)(tile_keys, jnp.arange(tile_total, dtype=jnp.int32))


def draw_counts(key, part):
    tile_total = TILES_DEV * N_DOM
    key_crowd, key_high, key_low = jax.random.split(jax.random.fold_in(key, 5), 3)
    crowded = jax.random.randint(key_crowd, (N_DOM,), 0, 3) == 0
    high_count = jax.random.randint(key_high, (tile_total,), 12, NEIGHBOURS + 1)
    low_count = jax.random.randint(key_low, (tile_total,), 5, 10)
    per_tile = jnp.repeat(crowded, TILES_DEV)
    result = jnp.where(per_tile, high_count, low_count)
    result = result.at[0].set(NEIGHBOURS).at[1].set(5)
    return result.astype(jnp.int32)


def draw_basis_vectors(key, part):
    row_total = TILES_DEV * N_DOM * TILE_ROWS
    normals = jax.random.normal(jax.random.fold_in(key, 7), (STORED + 1, row_total), jnp.float32)
    return (normals[1:] + 0.3 * normals[:-1]) / math.sqrt(1.09)


def setup_inputs(seed: int = 0) -> dict:
    arg_keys = jax.random.split(jax.random.key(seed), 5)
    return {
        "hessian": draw_hessian(jax.random.fold_in(arg_keys[4], 71), 0),
        "neighbours": draw_neighbours(jax.random.fold_in(arg_keys[4], 71), 0),
        "counts": draw_counts(jax.random.fold_in(arg_keys[4], 71), 0),
        "basis_vectors": draw_basis_vectors(jax.random.fold_in(arg_keys[4], 71), 0),
    }


finest = lax.Precision.HIGHEST

def neighbour_product(block_rows, hessian, neighbours, counts):
    col_count = block_rows.shape[0]
    tiled = block_rows.reshape(col_count, -1, TILE_ROWS)
    chosen = tiled[:, neighbours]
    live_mask = (jnp.arange(NEIGHBOURS)[None, :] < counts[:, None]).astype(jnp.float32)
    chosen = chosen * live_mask[None, :, :, None]
    result = jnp.einsum('tkij,btkj->bti', hessian, chosen, precision=finest)
    return result.reshape(col_count, -1)

def reference(hessian, neighbours, counts, basis_vectors):
    row_total = basis_vectors.shape[1]
    stored = basis_vectors
    current = basis_vectors[STORED - BLOCK:]
    blocks = []
    factors = []
    for lanczos_step in range(2):
        pending = neighbour_product(current, hessian, neighbours, counts)
        for sweep_index in range(2):
            coefficients = jnp.dot(stored, pending.T, precision=finest) / row_total
            pending = pending - jnp.dot(coefficients.T, stored, precision=finest)
        gram_block = jnp.dot(pending, pending.T, precision=finest) / row_total
        lower_factor = jnp.linalg.cholesky(gram_block)
        current = jax.scipy.linalg.solve_triangular(lower_factor, pending, lower=True)
        blocks.append(current)
        factors.append(lower_factor.T)
        stored = jnp.concatenate([current, stored[BLOCK:]], axis=0)
    return (jnp.stack(blocks), jnp.stack(factors))
```

```python
import jax
import jax.numpy as jnp
from jax import lax
from jax.experimental import pallas as pl
from jax.experimental.pallas import tpu as pltpu
from jax.sharding import PartitionSpec as P

BLOCK = 64
STORED = 512
N_DOM = 64
N_X, N_Z, N_CORE = 4, 8, 2
N_BLK = 4
OWN = BLOCK // N_BLK


high = lax.Precision.HIGH


def nt(a, b):
    return lax.dot_general(a, b, (((1,), (1,)), ((), ())), precision=high)


def nn(a, b):
    return lax.dot_general(a, b, (((1,), (0,)), ((), ())), precision=high)


def flipped(value, mask):
    return lax.ppermute(value, "dom", [(i, i ^ mask) for i in range(N_DOM)])


def along(value, axis, by):
    peers = lax.axis_size(axis)
    return lax.ppermute(value, axis, [(i, (i + by) % peers) for i in range(peers)])


def tree_sum(parts):
    while len(parts) > 1:
        parts = [parts[i] + parts[i + 1] for i in range(0, len(parts), 2)]
    return parts[0]


def summed(value, unit, count):
    return tree_sum([value] + [flipped(value, unit * k) for k in range(1, count)])


def part_of(value, index, size):
    return lax.dynamic_slice_in_dim(value, index * size, size, 0)


def scattered(value, place, unit, count):
    size = value.shape[0] // count
    parts = [part_of(value, place, size)]
    for k in range(1, count):
        parts.append(flipped(part_of(value, place ^ k, size), unit * k))
    return tree_sum(parts)


def collected(value, place, unit, count):
    size = value.shape[0]
    whole = jnp.zeros((size * count, *value.shape[1:]), value.dtype)
    whole = lax.dynamic_update_slice_in_dim(whole, value, place * size, 0)
    for k in range(1, count):
        whole = lax.dynamic_update_slice_in_dim(
            whole, flipped(value, unit * k), (place ^ k) * size, 0
        )
    return whole


def over_blk(value, me):
    whole = jnp.zeros((N_BLK, *value.shape), value.dtype)
    for k in range(N_BLK):
        piece = value if k == 0 else along(value, "blk", k)
        whole = lax.dynamic_update_slice_in_dim(whole, piece[None], (me - k) % N_BLK, 0)
    return whole


def over_blk_large(value, me):
    half = value.shape[0] // 2
    before = along(value, "blk", 1)
    after = along(value, "blk", -1)
    low = along(before[:half], "blk", 1)
    top = along(after[half:], "blk", -1)
    rows = value.shape[0]
    whole = jnp.zeros((N_BLK * rows, *value.shape[1:]), value.dtype)
    put = lax.dynamic_update_slice_in_dim
    whole = put(whole, value, me * rows, 0)
    whole = put(whole, before, (me - 1) % N_BLK * rows, 0)
    whole = put(whole, after, (me + 1) % N_BLK * rows, 0)
    whole = put(whole, low, (me + 2) % N_BLK * rows, 0)
    return put(whole, top, (me + 2) % N_BLK * rows + half, 0)


def factor_kernel(a_ref, o_ref):
    groups = BLOCK // 8
    lanes = 2 * BLOCK
    row_ids = lax.broadcasted_iota(jnp.int32, (8, lanes), 0)
    lane_ids = lax.broadcasted_iota(jnp.int32, (8, lanes), 1)
    a = [a_ref[8 * g : 8 * g + 8, :] for g in range(groups)]
    pivots = []
    for p in range(groups):
        cols = [
            [jnp.broadcast_to(a[g][:, 8 * p + c : 8 * p + c + 1], (8, lanes)) for g in range(p, groups)]
            for c in range(8)
        ]
        kept = jnp.zeros((8, lanes), jnp.float32)
        for c in range(8):
            pivot = jnp.broadcast_to(cols[c][0][c : c + 1, :], (8, lanes))
            kept = jnp.where(row_ids == c, pivot, kept)
            inverse = 1.0 / pivot
            row = jnp.broadcast_to(a[p][c : c + 1, :], (8, lanes))
            scale = [f * inverse for f in cols[c]]
            scale[0] = jnp.where(row_ids > c, scale[0], 0.0)
            for g in range(p, groups):
                a[g] = a[g] - scale[g - p] * row
            for later in range(c + 1, 8):
                level = jnp.broadcast_to(cols[later][0][c : c + 1, :], (8, lanes))
                cols[later] = [u - s * level for u, s in zip(cols[later], scale)]
        pivots.append(kept)
    for g in range(groups):
        scaled = a[g] * lax.rsqrt(pivots[g])
        o_ref[8 * g : 8 * g + 8, :] = jnp.where(lane_ids < row_ids + 8 * g, 0.0, scaled)


def factored(gram):
    wide = jnp.concatenate([gram, jnp.eye(BLOCK, dtype=jnp.float32)], axis=1)
    both = pl.pallas_call(
        factor_kernel,
        out_shape=jax.ShapeDtypeStruct((BLOCK, 2 * BLOCK), jnp.float32),
        in_specs=[pl.BlockSpec(memory_space=pltpu.VMEM)],
        out_specs=pl.BlockSpec(memory_space=pltpu.VMEM),
    )(wide)
    return both[:, :BLOCK], both[:, BLOCK:]


def neighbour_product(block_rows, hessian, neighbours, counts):
    me_dom = lax.axis_index("dom")
    tiles_own = hessian.shape[0]
    tile_rows = hessian.shape[2]
    col_count = block_rows.shape[0]
    pieces = [
        block_rows if offset == 0 else along(block_rows, "dom", offset)
        for offset in (2, 1, 0, -1, -2)
    ]
    extended = jnp.concatenate(pieces, axis=1).reshape(col_count, 5 * tiles_own, tile_rows)
    owner_dom = neighbours // tiles_own
    slot_index = (owner_dom - me_dom + 2) % N_DOM * tiles_own + neighbours % tiles_own
    chosen = jnp.take(extended, slot_index.reshape(-1), axis=1).reshape(
        col_count, tiles_own, neighbours.shape[1], tile_rows
    )
    live = (jnp.arange(neighbours.shape[1])[None, :] < counts[:, None]).astype(jnp.float32)
    chosen = chosen * live[None, :, :, None]
    result = jnp.einsum("tkij,btkj->bti", hessian, chosen, precision=high)
    return result.reshape(col_count, tiles_own * tile_rows)


def local(hessian, neighbours, counts, basis_vectors):
    me = lax.axis_index("blk")
    dom = lax.axis_index("dom")
    core, z, x = dom % N_CORE, dom // N_CORE % N_Z, dom // (N_CORE * N_Z)
    unit_z, unit_x = N_CORE, N_CORE * N_Z
    scale = 1.0 / (basis_vectors.shape[1] * N_DOM)

    arrived = [
        lax.ppermute(basis_vectors[BLOCK + OWN * k : BLOCK + OWN * (k + 1)], "blk", [(N_BLK - 1, k)])
        for k in range(N_BLK - 1)
    ]
    current = jnp.where(
        me == N_BLK - 1, basis_vectors[-OWN:], arrived[0] + arrived[1] + arrived[2]
    )
    stored = over_blk_large(basis_vectors, me)

    g = nt(basis_vectors, stored)
    g = scattered(g, core, 1, N_CORE)
    g = scattered(g, x, unit_x, N_X)
    g = summed(g, unit_z, N_Z)
    g = collected(g, x, unit_x, N_X)
    g = collected(g, core, 1, N_CORE)
    inner = over_blk_large(g, me) * scale

    blocks = []
    factors = []
    for step in range(2):
        product = neighbour_product(current, hessian, neighbours, counts)
        whole = over_blk(product, me).reshape(BLOCK, -1)
        part = nt(product, jnp.concatenate([stored, whole], axis=0))
        part = scattered(part, core, 1, N_CORE)
        part = summed(part, unit_x, N_X)
        part = summed(part, unit_z, N_Z)
        part = over_blk(part, me)
        half = OWN // N_CORE
        both = collected(part[None], core, 1, N_CORE)
        sums = both.transpose(1, 0, 2, 3).reshape(BLOCK, -1) * scale
        c, squares = sums[:, :STORED], sums[:, STORED:]
        d = 2.0 * c - nn(c, inner)
        f = c - nn(d, inner)
        gram = squares - nt(c, d) - nt(d, f)
        gram = 0.5 * (gram + gram.T)
        upper, inverse = factored(gram)
        new_block = nn(inverse, whole - nn(d, stored))
        current = part_of(new_block, me, OWN)
        blocks.append(current)
        factors.append(upper)
        if step == 0:
            crossed = nn(inverse, f)[:, BLOCK:]
            inner = jnp.concatenate(
                [
                    jnp.concatenate([jnp.eye(BLOCK, dtype=jnp.float32), crossed], axis=1),
                    jnp.concatenate([crossed.T, inner[BLOCK:, BLOCK:]], axis=1),
                ],
                axis=0,
            )
            stored = jnp.concatenate([new_block, stored[BLOCK:]], axis=0)
    return (jnp.stack(blocks), jnp.stack(factors))


def solution(mesh):
    placed = (P("dom", None, None, None), P("dom", None), P("dom"), P("blk", "dom"))
    return jax.shard_map(
        local, mesh=mesh, in_specs=placed, out_specs=(P(None, "blk", "dom"), P()), check_vma=False
    )
```

```python
import functools

import jax
import jax.numpy as jnp
from jax import lax
from jax.experimental import pallas as pl
from jax.experimental.pallas import tpu as pltpu
from jax.sharding import PartitionSpec as P

BLOCK = 64
STORED = 512
N_DOM = 64
N_X, N_Z, N_CORE = 4, 8, 2
N_BLK = 4
OWN = BLOCK // N_BLK
SPAN = 5


finest = lax.Precision.HIGHEST
bf16 = jnp.bfloat16
f32 = jnp.float32


def nt(a, b):
    return lax.dot_general(
        a, b, (((1,), (1,)), ((), ())), precision=finest, preferred_element_type=f32
    )


def nn(a, b):
    return lax.dot_general(
        a, b, (((1,), (0,)), ((), ())), precision=finest, preferred_element_type=f32
    )


def flipped(value, mask):
    return lax.ppermute(value, "dom", [(i, i ^ mask) for i in range(N_DOM)])


def along(value, axis, by):
    peers = lax.axis_size(axis)
    return lax.ppermute(value, axis, [(i, (i + by) % peers) for i in range(peers)])


def tree_sum(parts):
    while len(parts) > 1:
        parts = [parts[i] + parts[i + 1] for i in range(0, len(parts), 2)]
    return parts[0]


def summed(value, unit, steps):
    return tree_sum([value] + [flipped(value, unit * k) for k in steps])


VMEM = pl.BlockSpec(memory_space=pltpu.VMEM)
SMEM = pl.BlockSpec(memory_space=pltpu.SMEM)


def over_blk(low, top):
    up_low, down_top = along(low, "blk", 1), along(top, "blk", -1)
    up_top, down_low = along(top, "blk", 1), along(low, "blk", -1)
    far_low, far_top = along(up_low, "blk", 1), along(down_top, "blk", -1)
    return [low, top, down_low, down_top, far_low, far_top, up_low, up_top]


def split(value):
    top = value.astype(bf16)
    return top, (value - top.astype(f32)).astype(bf16)


CHUNK = 5


def product_kernel(slots_ref, hess_ref, *refs):
    pieces, out_ref, held, parts, result, sems = refs[:SPAN], *refs[SPAN:]
    tiles, listed, rows = held.shape[:3]
    chunks = listed // CHUNK

    def fetched(t, q):
        cut = pl.ds(CHUNK * q, CHUNK)
        return pltpu.make_async_copy(hess_ref.at[t, cut], held.at[t, cut], sems.at[t, q])

    for t in range(tiles):
        for q in range(chunks):
            fetched(t, q).start()
    for p in range(SPAN):
        values = pieces[p][...]
        for q in range(tiles):
            parts[tiles * p + q] = jnp.concatenate(
                split(values[:, rows * q : rows * (q + 1)]), axis=0
            )
    parts[SPAN * tiles] = jnp.zeros((2 * BLOCK, rows), bf16)
    dims = (((1,), (1,)), ((), ()))

    def tile(t, carry):
        first = jnp.zeros((2 * BLOCK, rows), f32)
        second = jnp.zeros((BLOCK, rows), f32)
        for k in range(listed):
            if k % CHUNK == 0:
                fetched(t, k // CHUNK).wait()
            x = parts[slots_ref[t * listed + k]]
            top, rest = split(held[t, k])
            first = first + lax.dot_general(x, top, dims, preferred_element_type=f32)
            second = second + lax.dot_general(x[:BLOCK], rest, dims, preferred_element_type=f32)
        result[t] = first[:BLOCK] + (first[BLOCK:] + second)
        return carry

    lax.fori_loop(0, tiles, tile, 0)
    out_ref[...] = jnp.concatenate([result[t] for t in range(tiles)], axis=1)


def neighbour_product(block, hessian, slots):
    tiles, listed, rows = hessian.shape[:3]
    pieces = [
        block if offset == 0 else along(block, "dom", offset) for offset in (2, 1, 0, -1, -2)
    ]
    return pl.pallas_call(
        product_kernel,
        out_shape=jax.ShapeDtypeStruct(block.shape, f32),
        grid_spec=pltpu.PrefetchScalarGridSpec(
            num_scalar_prefetch=1,
            grid=(),
            in_specs=[pl.BlockSpec(memory_space=pltpu.HBM)] + [VMEM] * SPAN,
            out_specs=VMEM,
            scratch_shapes=[
                pltpu.VMEM(hessian.shape, f32),
                pltpu.VMEM((SPAN * tiles + 1, 2 * BLOCK, rows), bf16),
                pltpu.VMEM((tiles, BLOCK, rows), f32),
                pltpu.SemaphoreType.DMA((tiles, listed // CHUNK)),
            ],
        ),
        compiler_params=pltpu.CompilerParams(vmem_limit_bytes=46 << 20),
        cost_estimate=pl.CostEstimate(flops=4 << 30, bytes_accessed=12 << 20, transcendentals=0),
        name="neighbour_product",
    )(slots, hessian, *pieces)


def eliminated(gram):
    groups = BLOCK // 8
    lanes = 2 * BLOCK
    row_ids = lax.broadcasted_iota(jnp.int32, (8, lanes), 0)
    lane_ids = lax.broadcasted_iota(jnp.int32, (8, lanes), 1)
    wide = jnp.concatenate([gram, jnp.zeros((BLOCK, BLOCK), f32)], axis=1)
    a = [
        wide[8 * g : 8 * g + 8, :] + jnp.where(lane_ids == row_ids + (8 * g + BLOCK), 1.0, 0.0)
        for g in range(groups)
    ]
    pivots = []
    for p in range(groups):
        cols = [
            [jnp.broadcast_to(a[g][:, 8 * p + c : 8 * p + c + 1], (8, lanes)) for g in range(p, groups)]
            for c in range(8)
        ]
        kept = jnp.zeros((8, lanes), f32)
        for c in range(8):
            pivot = jnp.broadcast_to(cols[c][0][c : c + 1, :], (8, lanes))
            kept = jnp.where(row_ids == c, pivot, kept)
            inverse = 1.0 / pivot
            row = jnp.broadcast_to(a[p][c : c + 1, :], (8, lanes))
            scale = [f * inverse for f in cols[c]]
            scale[0] = jnp.where(row_ids > c, scale[0], 0.0)
            for g in range(p, groups):
                a[g] = a[g] - scale[g - p] * row
            for later in range(c + 1, 8):
                level = jnp.broadcast_to(cols[later][0][c : c + 1, :], (8, lanes))
                cols[later] = [u - s * level for u, s in zip(cols[later], scale)]
        pivots.append(kept)
    return [
        jnp.where(lane_ids < row_ids + 8 * g, 0.0, a[g] * lax.rsqrt(pivots[g]))
        for g in range(groups)
    ]


def first_sums_kernel(place_ref, *refs):
    pieces, product_ref, stored_ref, out_ref = refs[:8], refs[8], refs[9], refs[10]
    me = place_ref[0]
    for k in range(8):
        row = ((me + k // 2) % N_BLK * 2 + k % 2) * BLOCK
        stored_ref[pl.ds(pl.multiple_of(row, BLOCK), BLOCK), :] = pieces[k][...]
    mine = jnp.concatenate([pieces[0][...], pieces[1][...]], axis=0)
    for o in range(3):
        other = jnp.concatenate([pieces[2 * o][...], pieces[2 * o + 1][...]], axis=0)
        g = nt(mine, other)
        for r in range(16):
            out_ref[16 * o + r] = g[8 * r : 8 * r + 8, :]
    own = product_ref[pl.ds(pl.multiple_of(me * OWN, OWN), OWN), :]
    c = nt(own, stored_ref[...])
    for h in range(2):
        for j in range(4):
            out_ref[48 + 4 * h + j] = c[8 * h : 8 * h + 8, 128 * j : 128 * j + 128]
    squares = nt(own, product_ref[...])
    out_ref[56] = jnp.concatenate([squares[:8], squares[8:]], axis=1)
    for q in range(57, 64):
        out_ref[q] = jnp.zeros((8, 128), f32)


def first_sums(place, pieces, product):
    return pl.pallas_call(
        first_sums_kernel,
        out_shape=[
            jax.ShapeDtypeStruct((STORED, product.shape[1]), f32),
            jax.ShapeDtypeStruct((N_DOM, 8, 128), f32),
        ],
        in_specs=[SMEM] + [VMEM] * 9,
        out_specs=[VMEM] * 2,
        compiler_params=pltpu.CompilerParams(vmem_limit_bytes=20 << 20),
        cost_estimate=pl.CostEstimate(flops=2 << 30, bytes_accessed=4 << 20, transcendentals=0),
        name="first_sums",
    )(place, *pieces, product)


def finished(c, squares, inner, product, stored, fresh=None):
    d = 2.0 * c - nn(c, inner)
    f = c - nn(d, inner)
    both = jnp.concatenate(eliminated(squares - nt(c, d) - nt(d, f)), axis=0)
    upper, inverse = both[:, :BLOCK], both[:, BLOCK:]
    if fresh is not None:
        product = product - nn(d[:, :BLOCK], fresh)
        d = jnp.where(lax.broadcasted_iota(jnp.int32, d.shape, 1) < BLOCK, 0.0, d)
    return nn(inverse, product - nn(d, stored)), upper, nn(inverse, f)


def first_block_kernel(scale, place_ref, *refs):
    pieces, product_ref, stored_ref = refs[:8], refs[8], refs[9]
    block_ref, upper_ref, inner_ref, held = refs[10:]
    me = place_ref[0]
    for k in range(8):
        held[((me + k // 2) % N_BLK) * 2 + k % 2] = pieces[k][...] * scale
    for i in range(N_BLK):
        for o in range(3):
            j = (i + o) % N_BLK
            g = [held[2 * i + (16 * o + r) // 32, (16 * o + r) % 32] for r in range(16)]
            g = jnp.concatenate(g, axis=0)
            inner_ref[128 * i : 128 * i + 128, 128 * j : 128 * j + 128] = g
            if o == 1:
                inner_ref[128 * j : 128 * j + 128, 128 * i : 128 * i + 128] = g.T
    c = jnp.concatenate(
        [
            jnp.concatenate([held[2 * i + 1, 16 + 4 * h + j] for j in range(4)], axis=1)
            for i in range(N_BLK)
            for h in range(2)
        ],
        axis=0,
    )
    squares = [held[2 * i + 1, 24] for i in range(N_BLK)]
    squares = jnp.concatenate([s[:, BLOCK * h : BLOCK * h + BLOCK] for s in squares for h in range(2)], axis=0)
    block_ref[...], upper_ref[...], crossed = finished(
        c, squares, inner_ref[...], product_ref[...], stored_ref[...]
    )
    rows = lax.broadcasted_iota(jnp.int32, crossed.shape, 0)
    lanes = lax.broadcasted_iota(jnp.int32, crossed.shape, 1)
    inner_ref[:BLOCK, :] = jnp.where(lanes < BLOCK, jnp.where(lanes == rows, 1.0, 0.0), crossed)
    inner_ref[BLOCK:, :BLOCK] = crossed.T[BLOCK:]


def first_block(place, pieces, product, stored, scale):
    shapes = [product.shape, (BLOCK, BLOCK), (STORED, STORED)]
    return pl.pallas_call(
        functools.partial(first_block_kernel, scale),
        out_shape=[jax.ShapeDtypeStruct(s, f32) for s in shapes],
        in_specs=[SMEM] + [VMEM] * 10,
        out_specs=[VMEM] * 3,
        scratch_shapes=[pltpu.VMEM((2 * N_BLK, N_DOM // 2, 8, 128), f32)],
        compiler_params=pltpu.CompilerParams(vmem_limit_bytes=24 << 20),
        cost_estimate=pl.CostEstimate(flops=2 << 30, bytes_accessed=6 << 20, transcendentals=0),
        name="first_block",
    )(place, *pieces, product, stored)


def second_sums_kernel(place_ref, product_ref, fresh_ref, stored_ref, kept_ref, sent_ref):
    me, core = place_ref[0], place_ref[1]
    for out_ref, which in ((kept_ref, core), (sent_ref, 1 - core)):
        own = product_ref[pl.ds(pl.multiple_of(me * OWN + which * 8, 8), 8), :]
        out_ref[:, :STORED] = nt(own, stored_ref[...])
        out_ref[:, :BLOCK] = nt(own, fresh_ref[...])
        out_ref[:, STORED:] = nt(own, product_ref[...])


def second_sums(place, product, fresh, stored):
    return pl.pallas_call(
        second_sums_kernel,
        out_shape=[jax.ShapeDtypeStruct((OWN // N_CORE, STORED + BLOCK), f32)] * 2,
        in_specs=[SMEM] + [VMEM] * 3,
        out_specs=[VMEM] * 2,
        compiler_params=pltpu.CompilerParams(vmem_limit_bytes=16 << 20),
        cost_estimate=pl.CostEstimate(flops=1 << 28, bytes_accessed=2 << 20, transcendentals=0),
        name="second_sums",
    )(place, product, fresh, stored)


def second_block_kernel(scale, place_ref, *refs):
    mine, others = refs[:4], refs[4]
    inner_ref, product_ref, stored_ref, fresh_ref, upper_ref = refs[5:10]
    blocks_ref, factors_ref, sums, whole = refs[10:]
    me, core = place_ref[0], place_ref[1]
    for k in range(N_BLK):
        row = (me + k) % N_BLK * OWN
        sums[pl.ds(pl.multiple_of(row + core * 8, 8), 8), :] = mine[k][...] * scale
        sums[pl.ds(pl.multiple_of(row + (1 - core) * 8, 8), 8), :] = others[k] * scale
    block, factors_ref[1], _ = finished(
        sums[:, :STORED],
        sums[:, STORED:],
        inner_ref[...],
        product_ref[...],
        stored_ref[...],
        fresh_ref[...],
    )
    whole[...] = block
    rows = pl.ds(pl.multiple_of(me * OWN, OWN), OWN)
    blocks_ref[0] = fresh_ref[rows, :]
    blocks_ref[1] = whole[rows, :]
    factors_ref[0] = upper_ref[...]


def second_block(place, mine, others, inner, product, stored, fresh, upper, scale):
    return pl.pallas_call(
        functools.partial(second_block_kernel, scale),
        out_shape=[
            jax.ShapeDtypeStruct((2, OWN, product.shape[1]), f32),
            jax.ShapeDtypeStruct((2, BLOCK, BLOCK), f32),
        ],
        in_specs=[SMEM] + [VMEM] * 10,
        out_specs=[VMEM] * 2,
        scratch_shapes=[
            pltpu.VMEM((BLOCK, STORED + BLOCK), f32),
            pltpu.VMEM(product.shape, f32),
        ],
        compiler_params=pltpu.CompilerParams(vmem_limit_bytes=24 << 20),
        cost_estimate=pl.CostEstimate(flops=2 << 30, bytes_accessed=6 << 20, transcendentals=0),
        name="second_block",
    )(place, *mine, others, inner, product, stored, fresh, upper)


def local(hessian, neighbours, counts, basis_vectors):
    me = lax.axis_index("blk")
    dom = lax.axis_index("dom")
    place = jnp.stack([me, dom % N_CORE]).astype(jnp.int32)
    unit_z, unit_x = N_CORE, N_CORE * N_Z
    tiles, listed = neighbours.shape
    scale = 1.0 / (basis_vectors.shape[1] * N_DOM)

    slots = (neighbours // tiles - dom + 2) % N_DOM * tiles + neighbours % tiles
    live = jnp.arange(listed)[None, :] < counts[:, None]
    slots = jnp.where(live, slots, SPAN * tiles).reshape(-1)

    low, top = basis_vectors[:BLOCK], basis_vectors[BLOCK:]
    arrived = [lax.ppermute(top, "blk", [(N_BLK - 1, k)]) for k in (0, 2, 1)]
    current = jnp.where(me == N_BLK - 1, top, arrived[0] + arrived[1] + arrived[2])
    current, low, top = lax.optimization_barrier((current, low, top))
    rows = over_blk(low, top)

    product = neighbour_product(current, hessian, slots)
    stored, pieces = first_sums(place, rows, product)
    pieces = lax.all_to_all(pieces, "dom", 0, 0, tiled=True)
    total = jnp.sum(pieces, axis=0)
    spread = lax.all_to_all(
        jnp.broadcast_to(total[None], pieces.shape), "dom", 0, 0, tiled=True
    )
    spread = over_blk(spread[: N_DOM // 2], spread[N_DOM // 2 :])
    first, upper, inner = first_block(place, spread, product, stored, scale)

    product = neighbour_product(first, hessian, slots)
    kept, sent = second_sums(place, product, first, stored)
    part = kept + flipped(sent, 1)
    part = summed(part, unit_x, (1, 2, 3))
    part = summed(part, unit_z, (1,))
    part = summed(part, unit_z, (2, 4, 6))
    mine = [part] + [along(part, "blk", -k) for k in (1, 2, 3)]
    others = flipped(jnp.stack(mine), 1)
    return second_block(place, mine, others, inner, product, stored, first, upper, scale)


def solution(mesh):
    placed = (P("dom", None, None, None), P("dom", None), P("dom"), P("blk", "dom"))
    return jax.shard_map(
        local, mesh=mesh, in_specs=placed, out_specs=(P(None, "blk", "dom"), P()), check_vma=False
    )
```

```python
import functools

import jax
import jax.numpy as jnp
from jax import lax
from jax.experimental import pallas as pl
from jax.experimental.pallas import tpu as pltpu
from jax.sharding import PartitionSpec as P

BLOCK = 64
STORED = 512
N_DOM = 64
N_X, N_Z, N_CORE = 4, 8, 2
N_BLK = 4
OWN = BLOCK // N_BLK
SPAN = 5
FETCH_LIMIT = 40
PRODUCT_LIMIT = 20


bf16 = jnp.bfloat16
f32 = jnp.float32


def split(value):
    top = value.astype(bf16)
    return top, (value - top.astype(f32)).astype(bf16)


def product_of(a, b, side):
    rows = a.shape[0]
    dims = (((1,), (side,)), ((), ()))
    a_top, a_rest = split(a)
    b_top, b_rest = split(b)
    both = lax.dot_general(
        jnp.concatenate([a_top, a_rest], axis=0), b_top, dims, preferred_element_type=f32
    )
    small = lax.dot_general(a_top, b_rest, dims, preferred_element_type=f32)
    return both[:rows] + (both[rows:] + small)


def nt(a, b):
    return product_of(a, b, 1)


def nn(a, b):
    return product_of(a, b, 0)


def flipped(value, mask):
    return lax.ppermute(value, "dom", [(i, i ^ mask) for i in range(N_DOM)])


def along(value, axis, by):
    peers = lax.axis_size(axis)
    return lax.ppermute(value, axis, [(i, (i + by) % peers) for i in range(peers)])


def tree_sum(parts):
    while len(parts) > 1:
        parts = [parts[i] + parts[i + 1] for i in range(0, len(parts), 2)]
    return parts[0]


def summed(value, unit, steps):
    return tree_sum([value] + [flipped(value, unit * k) for k in steps])


VMEM = pl.BlockSpec(memory_space=pltpu.VMEM)
SMEM = pl.BlockSpec(memory_space=pltpu.SMEM)


def over_blk(low, top):
    up_low, down_top = along(low, "blk", 1), along(top, "blk", -1)
    up_top, down_low = along(top, "blk", 1), along(low, "blk", -1)
    far_low, far_top = along(up_low, "blk", 1), along(down_top, "blk", -1)
    return [low, top, down_low, down_top, far_low, far_top, up_low, up_top]


def fetch_kernel(hess_ref, after_ref, out_ref, sems):
    tiles = hess_ref.shape[0]
    copies = [pltpu.make_async_copy(hess_ref.at[t], out_ref.at[t], sems.at[t]) for t in range(tiles)]
    for copy in copies:
        copy.start()
    for copy in copies:
        copy.wait()


def fetched(hessian, after):
    return pl.pallas_call(
        fetch_kernel,
        out_shape=pltpu.VMEM(hessian.shape, f32),
        in_specs=[pl.BlockSpec(memory_space=pltpu.HBM), VMEM],
        out_specs=VMEM,
        scratch_shapes=[pltpu.SemaphoreType.DMA((hessian.shape[0],))],
        compiler_params=pltpu.CompilerParams(vmem_limit_bytes=FETCH_LIMIT << 20),
        cost_estimate=pl.CostEstimate(flops=0, bytes_accessed=20 << 20, transcendentals=0),
        name="fetch",
    )(hessian, after)


def product_kernel(slots_ref, hess_ref, *refs):
    pieces, out_ref, parts, result = refs[:SPAN], *refs[SPAN:]
    tiles, listed, rows = hess_ref.shape[:3]
    for p in range(SPAN):
        values = pieces[p][...]
        for q in range(tiles):
            parts[tiles * p + q] = jnp.concatenate(
                split(values[:, rows * q : rows * (q + 1)]), axis=0
            )
    parts[SPAN * tiles] = jnp.zeros((2 * BLOCK, rows), bf16)
    dims = (((1,), (1,)), ((), ()))

    def tile(t, carry):
        first = jnp.zeros((2 * BLOCK, rows), f32)
        second = jnp.zeros((BLOCK, rows), f32)
        for k in range(listed):
            x = parts[slots_ref[t * listed + k]]
            top, rest = split(hess_ref[t, k])
            first = first + lax.dot_general(x, top, dims, preferred_element_type=f32)
            second = second + lax.dot_general(x[:BLOCK], rest, dims, preferred_element_type=f32)
        result[t] = first[:BLOCK] + (first[BLOCK:] + second)
        return carry

    lax.fori_loop(0, tiles, tile, 0)
    out_ref[...] = jnp.concatenate([result[t] for t in range(tiles)], axis=1)


def neighbour_product(block, hessian, slots, after):
    tiles, rows = hessian.shape[0], hessian.shape[2]
    pieces = [
        block if offset == 0 else along(block, "dom", offset) for offset in (2, 1, 0, -1, -2)
    ]
    return pl.pallas_call(
        product_kernel,
        out_shape=jax.ShapeDtypeStruct(block.shape, f32),
        grid_spec=pltpu.PrefetchScalarGridSpec(
            num_scalar_prefetch=1,
            grid=(),
            in_specs=[VMEM] * (1 + SPAN),
            out_specs=VMEM,
            scratch_shapes=[
                pltpu.VMEM((SPAN * tiles + 1, 2 * BLOCK, rows), bf16),
                pltpu.VMEM((tiles, BLOCK, rows), f32),
            ],
        ),
        compiler_params=pltpu.CompilerParams(vmem_limit_bytes=PRODUCT_LIMIT << 20),
        cost_estimate=pl.CostEstimate(flops=4 << 30, bytes_accessed=12 << 20, transcendentals=0),
        name="neighbour_product",
    )(slots, fetched(hessian, after), *pieces)


def eliminated(gram):
    groups = BLOCK // 8
    lanes = 2 * BLOCK
    row_ids = lax.broadcasted_iota(jnp.int32, (8, lanes), 0)
    lane_ids = lax.broadcasted_iota(jnp.int32, (8, lanes), 1)
    wide = jnp.concatenate([gram, jnp.zeros((BLOCK, BLOCK), f32)], axis=1)
    a = [
        wide[8 * g : 8 * g + 8, :] + jnp.where(lane_ids == row_ids + (8 * g + BLOCK), 1.0, 0.0)
        for g in range(groups)
    ]
    pivots = []
    for p in range(groups):
        cols = [
            [jnp.broadcast_to(a[g][:, 8 * p + c : 8 * p + c + 1], (8, lanes)) for g in range(p, groups)]
            for c in range(8)
        ]
        kept = jnp.zeros((8, lanes), f32)
        for c in range(8):
            pivot = jnp.broadcast_to(cols[c][0][c : c + 1, :], (8, lanes))
            kept = jnp.where(row_ids == c, pivot, kept)
            inverse = 1.0 / pivot
            row = jnp.broadcast_to(a[p][c : c + 1, :], (8, lanes))
            scale = [f * inverse for f in cols[c]]
            scale[0] = jnp.where(row_ids > c, scale[0], 0.0)
            for g in range(p, groups):
                a[g] = a[g] - scale[g - p] * row
            for later in range(c + 1, 8):
                level = jnp.broadcast_to(cols[later][0][c : c + 1, :], (8, lanes))
                cols[later] = [u - s * level for u, s in zip(cols[later], scale)]
        pivots.append(kept)
    return [
        jnp.where(lane_ids < row_ids + 8 * g, 0.0, a[g] * lax.rsqrt(pivots[g]))
        for g in range(groups)
    ]


def first_sums_kernel(place_ref, *refs):
    pieces, product_ref, stored_ref, out_ref = refs[:8], refs[8], refs[9], refs[10]
    me = place_ref[0]
    for k in range(8):
        row = ((me + k // 2) % N_BLK * 2 + k % 2) * BLOCK
        stored_ref[pl.ds(pl.multiple_of(row, BLOCK), BLOCK), :] = pieces[k][...]
    mine = jnp.concatenate([pieces[0][...], pieces[1][...]], axis=0)
    for o in range(3):
        other = jnp.concatenate([pieces[2 * o][...], pieces[2 * o + 1][...]], axis=0)
        g = nt(mine, other)
        for r in range(16):
            out_ref[16 * o + r] = g[8 * r : 8 * r + 8, :]
    own = product_ref[pl.ds(pl.multiple_of(me * OWN, OWN), OWN), :]
    c = nt(own, stored_ref[...])
    for h in range(2):
        for j in range(4):
            out_ref[48 + 4 * h + j] = c[8 * h : 8 * h + 8, 128 * j : 128 * j + 128]
    squares = nt(own, product_ref[...])
    out_ref[56] = jnp.concatenate([squares[:8], squares[8:]], axis=1)
    for q in range(57, 64):
        out_ref[q] = jnp.zeros((8, 128), f32)


def first_sums(place, pieces, product):
    return pl.pallas_call(
        first_sums_kernel,
        out_shape=[
            jax.ShapeDtypeStruct((STORED, product.shape[1]), f32),
            jax.ShapeDtypeStruct((N_DOM, 8, 128), f32),
        ],
        in_specs=[SMEM] + [VMEM] * 9,
        out_specs=[VMEM] * 2,
        compiler_params=pltpu.CompilerParams(vmem_limit_bytes=20 << 20),
        cost_estimate=pl.CostEstimate(flops=2 << 30, bytes_accessed=4 << 20, transcendentals=0),
        name="first_sums",
    )(place, *pieces, product)


def finished(c, squares, inner, product, stored, fresh=None):
    d = 2.0 * c - nn(c, inner)
    f = c - nn(d, inner)
    both = jnp.concatenate(eliminated(squares - nt(c, d) - nt(d, f)), axis=0)
    upper, inverse = both[:, :BLOCK], both[:, BLOCK:]
    if fresh is not None:
        product = product - nn(d[:, :BLOCK], fresh)
        d = jnp.where(lax.broadcasted_iota(jnp.int32, d.shape, 1) < BLOCK, 0.0, d)
    return nn(inverse, product - nn(d, stored)), upper, nn(inverse, f)


def first_block_kernel(scale, place_ref, *refs):
    pieces, product_ref, stored_ref = refs[:8], refs[8], refs[9]
    block_ref, upper_ref, inner_ref, held = refs[10:]
    me = place_ref[0]
    for k in range(8):
        held[((me + k // 2) % N_BLK) * 2 + k % 2] = pieces[k][...] * scale
    for i in range(N_BLK):
        for o in range(3):
            j = (i + o) % N_BLK
            g = [held[2 * i + (16 * o + r) // 32, (16 * o + r) % 32] for r in range(16)]
            g = jnp.concatenate(g, axis=0)
            inner_ref[128 * i : 128 * i + 128, 128 * j : 128 * j + 128] = g
            if o == 1:
                inner_ref[128 * j : 128 * j + 128, 128 * i : 128 * i + 128] = g.T
    c = jnp.concatenate(
        [
            jnp.concatenate([held[2 * i + 1, 16 + 4 * h + j] for j in range(4)], axis=1)
            for i in range(N_BLK)
            for h in range(2)
        ],
        axis=0,
    )
    squares = [held[2 * i + 1, 24] for i in range(N_BLK)]
    squares = jnp.concatenate([s[:, BLOCK * h : BLOCK * h + BLOCK] for s in squares for h in range(2)], axis=0)
    block_ref[...], upper_ref[...], crossed = finished(
        c, squares, inner_ref[...], product_ref[...], stored_ref[...]
    )
    rows = lax.broadcasted_iota(jnp.int32, crossed.shape, 0)
    lanes = lax.broadcasted_iota(jnp.int32, crossed.shape, 1)
    inner_ref[:BLOCK, :] = jnp.where(lanes < BLOCK, jnp.where(lanes == rows, 1.0, 0.0), crossed)
    inner_ref[BLOCK:, :BLOCK] = crossed.T[BLOCK:]


def first_block(place, pieces, product, stored, scale):
    shapes = [product.shape, (BLOCK, BLOCK), (STORED, STORED)]
    return pl.pallas_call(
        functools.partial(first_block_kernel, scale),
        out_shape=[jax.ShapeDtypeStruct(s, f32) for s in shapes],
        in_specs=[SMEM] + [VMEM] * 10,
        out_specs=[VMEM] * 3,
        scratch_shapes=[pltpu.VMEM((2 * N_BLK, N_DOM // 2, 8, 128), f32)],
        compiler_params=pltpu.CompilerParams(vmem_limit_bytes=24 << 20),
        cost_estimate=pl.CostEstimate(flops=2 << 30, bytes_accessed=6 << 20, transcendentals=0),
        name="first_block",
    )(place, *pieces, product, stored)


def second_sums_kernel(place_ref, product_ref, fresh_ref, stored_ref, kept_ref, sent_ref, sums):
    me, core = place_ref[0], place_ref[1]
    own = product_ref[pl.ds(pl.multiple_of(me * OWN, OWN), OWN), :]
    sums[:, :STORED] = nt(own, stored_ref[...])
    sums[:, :BLOCK] = nt(own, fresh_ref[...])
    sums[:, STORED:] = nt(own, product_ref[...])
    half = OWN // N_CORE
    kept_ref[...] = sums[pl.ds(pl.multiple_of(core * half, half), half), :]
    sent_ref[...] = sums[pl.ds(pl.multiple_of((1 - core) * half, half), half), :]


def second_sums(place, product, fresh, stored):
    return pl.pallas_call(
        second_sums_kernel,
        out_shape=[jax.ShapeDtypeStruct((OWN // N_CORE, STORED + BLOCK), f32)] * 2,
        in_specs=[SMEM] + [VMEM] * 3,
        out_specs=[VMEM] * 2,
        scratch_shapes=[pltpu.VMEM((OWN, STORED + BLOCK), f32)],
        compiler_params=pltpu.CompilerParams(vmem_limit_bytes=16 << 20),
        cost_estimate=pl.CostEstimate(flops=1 << 28, bytes_accessed=2 << 20, transcendentals=0),
        name="second_sums",
    )(place, product, fresh, stored)


def second_block_kernel(scale, place_ref, *refs):
    mine, others = refs[:4], refs[4]
    inner_ref, product_ref, stored_ref, fresh_ref, upper_ref = refs[5:10]
    blocks_ref, factors_ref, sums, whole = refs[10:]
    me, core = place_ref[0], place_ref[1]
    for k in range(N_BLK):
        row = (me + k) % N_BLK * OWN
        sums[pl.ds(pl.multiple_of(row + core * 8, 8), 8), :] = mine[k][...] * scale
        sums[pl.ds(pl.multiple_of(row + (1 - core) * 8, 8), 8), :] = others[k] * scale
    block, factors_ref[1], _ = finished(
        sums[:, :STORED],
        sums[:, STORED:],
        inner_ref[...],
        product_ref[...],
        stored_ref[...],
        fresh_ref[...],
    )
    whole[...] = block
    rows = pl.ds(pl.multiple_of(me * OWN, OWN), OWN)
    blocks_ref[0] = fresh_ref[rows, :]
    blocks_ref[1] = whole[rows, :]
    factors_ref[0] = upper_ref[...]


def second_block(place, mine, others, inner, product, stored, fresh, upper, scale):
    return pl.pallas_call(
        functools.partial(second_block_kernel, scale),
        out_shape=[
            jax.ShapeDtypeStruct((2, OWN, product.shape[1]), f32),
            jax.ShapeDtypeStruct((2, BLOCK, BLOCK), f32),
        ],
        in_specs=[SMEM] + [VMEM] * 10,
        out_specs=[VMEM] * 2,
        scratch_shapes=[
            pltpu.VMEM((BLOCK, STORED + BLOCK), f32),
            pltpu.VMEM(product.shape, f32),
        ],
        compiler_params=pltpu.CompilerParams(vmem_limit_bytes=24 << 20),
        cost_estimate=pl.CostEstimate(flops=2 << 30, bytes_accessed=6 << 20, transcendentals=0),
        name="second_block",
    )(place, *mine, others, inner, product, stored, fresh, upper)


def local(hessian, neighbours, counts, basis_vectors):
    me = lax.axis_index("blk")
    dom = lax.axis_index("dom")
    place = jnp.stack([me, dom % N_CORE]).astype(jnp.int32)
    unit_z, unit_x = N_CORE, N_CORE * N_Z
    tiles, listed = neighbours.shape
    scale = 1.0 / (basis_vectors.shape[1] * N_DOM)

    slots = (neighbours // tiles - dom + 2) % N_DOM * tiles + neighbours % tiles
    live = jnp.arange(listed)[None, :] < counts[:, None]
    slots = jnp.where(live, slots, SPAN * tiles).reshape(-1)

    low, top = basis_vectors[:BLOCK], basis_vectors[BLOCK:]
    up_top, down_top = along(top, "blk", 1), along(top, "blk", -1)
    one, two, low = lax.optimization_barrier((up_top[: BLOCK // 2], down_top[BLOCK // 2 :], low))
    far_one, far_two = along(one, "blk", 1), along(two, "blk", -1)
    far_top = jnp.concatenate([far_one, far_two], axis=0)
    current = jnp.where(
        me < 2, jnp.where(me == 0, up_top, far_top), jnp.where(me == 2, down_top, top)
    )
    up_low, down_low = along(low, "blk", 1), along(low, "blk", -1)
    far_low = jnp.concatenate(
        [along(up_low[: BLOCK // 2], "blk", 1), along(down_low[BLOCK // 2 :], "blk", -1)], axis=0
    )
    rows = [low, top, down_low, down_top, far_low, far_top, up_low, up_top]

    product = neighbour_product(current, hessian, slots, current)
    stored, pieces = first_sums(place, rows, product)
    pieces = lax.all_to_all(pieces, "dom", 0, 0, tiled=True)
    total = jnp.sum(pieces, axis=0)
    spread = lax.all_to_all(
        jnp.broadcast_to(total[None], pieces.shape), "dom", 0, 0, tiled=True
    )
    spread = over_blk(spread[: N_DOM // 2], spread[N_DOM // 2 :])
    first, upper, inner = first_block(place, spread, product, stored, scale)

    product = neighbour_product(first, hessian, slots, first)
    kept, sent = second_sums(place, product, first, stored)
    part = kept + flipped(sent, 1)
    part = summed(part, unit_x, (1, 2, 3))
    part = summed(part, unit_z, (1,))
    part = summed(part, unit_z, (2, 4, 6))
    mine = [part] + [along(part, "blk", -k) for k in (1, 2, 3)]
    others = flipped(jnp.stack(mine), 1)
    return second_block(place, mine, others, inner, product, stored, first, upper, scale)


def solution(mesh):
    placed = (P("dom", None, None, None), P("dom", None), P("dom"), P("blk", "dom"))
    return jax.shard_map(
        local, mesh=mesh, in_specs=placed, out_specs=(P(None, "blk", "dom"), P()), check_vma=False
    )
```

```python
import functools

import jax
import jax.numpy as jnp
from jax import lax
from jax.experimental import pallas as pl
from jax.experimental.pallas import tpu as pltpu
from jax.sharding import PartitionSpec as P

BLOCK = 64
STORED = 512
N_DOM = 64
N_X, N_Z, N_CORE = 4, 8, 2
N_BLK = 4
OWN = BLOCK // N_BLK
SPAN = 6
FETCH_LIMIT = 40
PRODUCT_LIMIT = 20


bf16 = jnp.bfloat16
f32 = jnp.float32


def split(value):
    top = value.astype(bf16)
    return top, (value - top.astype(f32)).astype(bf16)


def product_of(a, b, side):
    rows = a.shape[0]
    dims = (((1,), (side,)), ((), ()))
    a_top, a_rest = split(a)
    b_top, b_rest = split(b)
    both = lax.dot_general(
        jnp.concatenate([a_top, a_rest], axis=0), b_top, dims, preferred_element_type=f32
    )
    small = lax.dot_general(a_top, b_rest, dims, preferred_element_type=f32)
    return both[:rows] + (both[rows:] + small)


def exactly(a, b, side):
    return lax.dot_general(
        a,
        b,
        (((1,), (side,)), ((), ())),
        precision=lax.Precision.HIGHEST,
        preferred_element_type=f32,
    )


def nt(a, b):
    return product_of(a, b, 1)


def nn(a, b):
    return product_of(a, b, 0)


def flipped(value, mask):
    return lax.ppermute(value, "dom", [(i, i ^ mask) for i in range(N_DOM)])


def along(value, axis, by):
    peers = lax.axis_size(axis)
    return lax.ppermute(value, axis, [(i, (i + by) % peers) for i in range(peers)])


def tree_sum(parts):
    while len(parts) > 1:
        parts = [parts[i] + parts[i + 1] for i in range(0, len(parts), 2)]
    return parts[0]


def summed(value, unit, steps):
    return tree_sum([value] + [flipped(value, unit * k) for k in steps])


VMEM = pl.BlockSpec(memory_space=pltpu.VMEM)
SMEM = pl.BlockSpec(memory_space=pltpu.SMEM)


def over_blk(low, top):
    up_low, down_top = along(low, "blk", 1), along(top, "blk", -1)
    up_top, down_low = along(top, "blk", 1), along(low, "blk", -1)
    far_low, far_top = along(up_low, "blk", 1), along(down_top, "blk", -1)
    return [low, top, down_low, down_top, far_low, far_top, up_low, up_top]


def fetch_kernel(hess_ref, after_ref, out_ref, sems):
    tiles = hess_ref.shape[0]
    copies = [pltpu.make_async_copy(hess_ref.at[t], out_ref.at[t], sems.at[t]) for t in range(tiles)]
    for copy in copies:
        copy.start()
    for copy in copies:
        copy.wait()


def fetched(hessian, after):
    return pl.pallas_call(
        fetch_kernel,
        out_shape=pltpu.VMEM(hessian.shape, f32),
        in_specs=[pl.BlockSpec(memory_space=pltpu.HBM), VMEM],
        out_specs=VMEM,
        scratch_shapes=[pltpu.SemaphoreType.DMA((hessian.shape[0],))],
        compiler_params=pltpu.CompilerParams(vmem_limit_bytes=FETCH_LIMIT << 20),
        cost_estimate=pl.CostEstimate(flops=0, bytes_accessed=20 << 20, transcendentals=0),
        name="fetch",
    )(hessian, after)


def product_kernel(slots_ref, hess_ref, *refs):
    pieces, out_ref, parts, result = refs[:SPAN], *refs[SPAN:]
    tiles, listed, rows = hess_ref.shape[:3]
    for p in range(SPAN):
        values = pieces[p][...]
        for q in range(tiles):
            parts[tiles * p + q] = jnp.concatenate(
                split(values[:, rows * q : rows * (q + 1)]), axis=0
            )
    parts[SPAN * tiles] = jnp.zeros((2 * BLOCK, rows), bf16)
    dims = (((1,), (1,)), ((), ()))

    def tile(t, carry):
        first = jnp.zeros((2 * BLOCK, rows), f32)
        second = jnp.zeros((BLOCK, rows), f32)
        for k in range(listed):
            x = parts[slots_ref[t * listed + k]]
            top, rest = split(hess_ref[t, k])
            first = first + lax.dot_general(x, top, dims, preferred_element_type=f32)
            second = second + lax.dot_general(x[:BLOCK], rest, dims, preferred_element_type=f32)
        result[t] = first[:BLOCK] + (first[BLOCK:] + second)
        return carry

    lax.fori_loop(0, tiles, tile, 0)
    out_ref[...] = jnp.concatenate([result[t] for t in range(tiles)], axis=1)


def neighbour_product(block, hessian, slots):
    tiles, rows = hessian.shape[0], hessian.shape[2]
    before, after = along(block, "dom", 2), along(block, "dom", -2)
    partner = flipped(block, 1)
    before, after, held = lax.optimization_barrier((before, after, fetched(hessian, block)))
    evens = [(i, i + 1) for i in range(0, N_DOM, 2)]
    pieces = [
        before,
        lax.ppermute(before, "dom", [(j, i) for i, j in evens]),
        block,
        partner,
        after,
        lax.ppermute(after, "dom", evens),
    ]
    return pl.pallas_call(
        product_kernel,
        out_shape=jax.ShapeDtypeStruct(block.shape, f32),
        grid_spec=pltpu.PrefetchScalarGridSpec(
            num_scalar_prefetch=1,
            grid=(),
            in_specs=[VMEM] * (1 + SPAN),
            out_specs=VMEM,
            scratch_shapes=[
                pltpu.VMEM((SPAN * tiles + 1, 2 * BLOCK, rows), bf16),
                pltpu.VMEM((tiles, BLOCK, rows), f32),
            ],
        ),
        compiler_params=pltpu.CompilerParams(vmem_limit_bytes=PRODUCT_LIMIT << 20),
        cost_estimate=pl.CostEstimate(flops=4 << 30, bytes_accessed=12 << 20, transcendentals=0),
        name="neighbour_product",
    )(slots, held, *pieces)


def eliminated(gram):
    groups = BLOCK // 8
    lanes = 2 * BLOCK
    row_ids = lax.broadcasted_iota(jnp.int32, (8, lanes), 0)
    lane_ids = lax.broadcasted_iota(jnp.int32, (8, lanes), 1)
    wide = jnp.concatenate([gram, jnp.zeros((BLOCK, BLOCK), f32)], axis=1)
    a = [
        wide[8 * g : 8 * g + 8, :] + jnp.where(lane_ids == row_ids + (8 * g + BLOCK), 1.0, 0.0)
        for g in range(groups)
    ]
    pivots = []
    for p in range(groups):
        cols = [
            [jnp.broadcast_to(a[g][:, 8 * p + c : 8 * p + c + 1], (8, lanes)) for g in range(p, groups)]
            for c in range(8)
        ]
        kept = jnp.zeros((8, lanes), f32)
        for c in range(8):
            pivot = jnp.broadcast_to(cols[c][0][c : c + 1, :], (8, lanes))
            kept = jnp.where(row_ids == c, pivot, kept)
            inverse = 1.0 / pivot
            row = jnp.broadcast_to(a[p][c : c + 1, :], (8, lanes))
            scale = [f * inverse for f in cols[c]]
            scale[0] = jnp.where(row_ids > c, scale[0], 0.0)
            for g in range(p, groups):
                a[g] = a[g] - scale[g - p] * row
            for later in range(c + 1, 8):
                level = jnp.broadcast_to(cols[later][0][c : c + 1, :], (8, lanes))
                cols[later] = [u - s * level for u, s in zip(cols[later], scale)]
        pivots.append(kept)
    return [
        jnp.where(lane_ids < row_ids + 8 * g, 0.0, a[g] * lax.rsqrt(pivots[g]))
        for g in range(groups)
    ]


def first_sums_kernel(place_ref, *refs):
    mine, after, before = [
        jnp.concatenate([refs[2 * k][...], refs[2 * k + 1][...]], axis=0) for k in range(3)
    ]
    product_ref, out_ref = refs[6], refs[7]
    for o, (a, b) in enumerate(((mine, mine), (mine, after), (before, after))):
        g = nt(a, b)
        for r in range(16):
            out_ref[16 * o + r] = g[8 * r : 8 * r + 8, :]
    c = nt(product_ref[...], mine)
    for h in range(8):
        out_ref[48 + h] = c[8 * h : 8 * h + 8, :]
    own = product_ref[pl.ds(pl.multiple_of(place_ref[0] * OWN, OWN), OWN), :]
    squares = nt(own, product_ref[...])
    out_ref[56] = jnp.concatenate([squares[:8], squares[8:]], axis=1)
    for q in range(57, 64):
        out_ref[q] = jnp.zeros((8, 128), f32)


def first_sums(place, pieces, product):
    return pl.pallas_call(
        first_sums_kernel,
        out_shape=jax.ShapeDtypeStruct((N_DOM, 8, 128), f32),
        in_specs=[SMEM] + [VMEM] * 7,
        out_specs=VMEM,
        compiler_params=pltpu.CompilerParams(vmem_limit_bytes=20 << 20),
        cost_estimate=pl.CostEstimate(flops=2 << 30, bytes_accessed=4 << 20, transcendentals=0),
        name="first_sums",
    )(place, *pieces, product)


def ordered_kernel(place_ref, *refs):
    for k in range(8):
        row = ((place_ref[0] + k // 2) % N_BLK * 2 + k % 2) * BLOCK
        refs[8][pl.ds(pl.multiple_of(row, BLOCK), BLOCK), :] = refs[k][...]


def ordered(place, pieces):
    return pl.pallas_call(
        ordered_kernel,
        out_shape=jax.ShapeDtypeStruct((STORED, pieces[0].shape[1]), f32),
        in_specs=[SMEM] + [VMEM] * 8,
        out_specs=VMEM,
        compiler_params=pltpu.CompilerParams(vmem_limit_bytes=16 << 20),
        cost_estimate=pl.CostEstimate(flops=0, bytes_accessed=3 << 20, transcendentals=0),
        name="ordered",
    )(place, *pieces)


def finished(c, squares, inner, product, stored, fresh=None):
    d = 2.0 * c - exactly(c, inner, 0)
    f = c - exactly(d, inner, 0)
    both = jnp.concatenate(eliminated(squares - exactly(c, d, 1) - exactly(d, f, 1)), axis=0)
    upper, inverse = both[:, :BLOCK], both[:, BLOCK:]
    if fresh is not None:
        product = product - nn(d[:, :BLOCK], fresh)
        d = jnp.where(lax.broadcasted_iota(jnp.int32, d.shape, 1) < BLOCK, 0.0, d)
    return nn(inverse, product - nn(d, stored)), upper, nn(inverse, f)


def first_block_kernel(scale, place_ref, *refs):
    pieces, product_ref, stored_ref = refs[:8], refs[8], refs[9]
    block_ref, upper_ref, inner_ref, held = refs[10:]
    me = place_ref[0]
    for k in range(8):
        held[((me + k // 2) % N_BLK) * 2 + k % 2] = pieces[k][...] * scale
    for b in range(N_BLK):
        for o, (i, j) in enumerate(((b, b), (b, b + 1), (b - 1, b + 1))):
            i, j = 128 * (i % N_BLK), 128 * (j % N_BLK)
            g = [held[2 * b + (16 * o + r) // 32, (16 * o + r) % 32] for r in range(16)]
            g = jnp.concatenate(g, axis=0)
            inner_ref[i : i + 128, j : j + 128] = g
            if o == 1:
                inner_ref[j : j + 128, i : i + 128] = g.T
    c = jnp.concatenate(
        [
            jnp.concatenate([held[2 * b + 1, 16 + h] for b in range(N_BLK)], axis=1)
            for h in range(8)
        ],
        axis=0,
    )
    squares = [held[2 * i + 1, 24] for i in range(N_BLK)]
    squares = jnp.concatenate([s[:, BLOCK * h : BLOCK * h + BLOCK] for s in squares for h in range(2)], axis=0)
    block_ref[...], upper_ref[...], crossed = finished(
        c, squares, inner_ref[...], product_ref[...], stored_ref[...]
    )
    rows = lax.broadcasted_iota(jnp.int32, crossed.shape, 0)
    lanes = lax.broadcasted_iota(jnp.int32, crossed.shape, 1)
    inner_ref[:BLOCK, :] = jnp.where(lanes < BLOCK, jnp.where(lanes == rows, 1.0, 0.0), crossed)
    inner_ref[BLOCK:, :BLOCK] = crossed.T[BLOCK:]


def first_block(place, pieces, product, stored, scale):
    shapes = [product.shape, (BLOCK, BLOCK), (STORED, STORED)]
    return pl.pallas_call(
        functools.partial(first_block_kernel, scale),
        out_shape=[jax.ShapeDtypeStruct(s, f32) for s in shapes],
        in_specs=[SMEM] + [VMEM] * 10,
        out_specs=[VMEM] * 3,
        scratch_shapes=[pltpu.VMEM((2 * N_BLK, N_DOM // 2, 8, 128), f32)],
        compiler_params=pltpu.CompilerParams(vmem_limit_bytes=24 << 20),
        cost_estimate=pl.CostEstimate(flops=2 << 30, bytes_accessed=6 << 20, transcendentals=0),
        name="first_block",
    )(place, *pieces, product, stored)


def second_sums_kernel(place_ref, product_ref, fresh_ref, stored_ref, kept_ref, sent_ref, sums):
    me, core = place_ref[0], place_ref[1]
    own = product_ref[pl.ds(pl.multiple_of(me * OWN, OWN), OWN), :]
    sums[:, :STORED] = nt(own, stored_ref[...])
    sums[:, :BLOCK] = nt(own, fresh_ref[...])
    sums[:, STORED:] = nt(own, product_ref[...])
    half = OWN // N_CORE
    kept_ref[...] = sums[pl.ds(pl.multiple_of(core * half, half), half), :]
    sent_ref[...] = sums[pl.ds(pl.multiple_of((1 - core) * half, half), half), :]


def second_sums(place, product, fresh, stored):
    return pl.pallas_call(
        second_sums_kernel,
        out_shape=[jax.ShapeDtypeStruct((OWN // N_CORE, STORED + BLOCK), f32)] * 2,
        in_specs=[SMEM] + [VMEM] * 3,
        out_specs=[VMEM] * 2,
        scratch_shapes=[pltpu.VMEM((OWN, STORED + BLOCK), f32)],
        compiler_params=pltpu.CompilerParams(vmem_limit_bytes=16 << 20),
        cost_estimate=pl.CostEstimate(flops=1 << 28, bytes_accessed=2 << 20, transcendentals=0),
        name="second_sums",
    )(place, product, fresh, stored)


def second_block_kernel(scale, place_ref, *refs):
    mine, others = refs[:4], refs[4]
    inner_ref, product_ref, stored_ref, fresh_ref, upper_ref = refs[5:10]
    blocks_ref, factors_ref, sums, whole = refs[10:]
    me, core = place_ref[0], place_ref[1]
    for k in range(N_BLK):
        row = (me + k) % N_BLK * OWN
        sums[pl.ds(pl.multiple_of(row + core * 8, 8), 8), :] = mine[k][...] * scale
        sums[pl.ds(pl.multiple_of(row + (1 - core) * 8, 8), 8), :] = others[k] * scale
    block, factors_ref[1], _ = finished(
        sums[:, :STORED],
        sums[:, STORED:],
        inner_ref[...],
        product_ref[...],
        stored_ref[...],
        fresh_ref[...],
    )
    whole[...] = block
    rows = pl.ds(pl.multiple_of(me * OWN, OWN), OWN)
    blocks_ref[0] = fresh_ref[rows, :]
    blocks_ref[1] = whole[rows, :]
    factors_ref[0] = upper_ref[...]


def second_block(place, mine, others, inner, product, stored, fresh, upper, scale):
    return pl.pallas_call(
        functools.partial(second_block_kernel, scale),
        out_shape=[
            jax.ShapeDtypeStruct((2, OWN, product.shape[1]), f32),
            jax.ShapeDtypeStruct((2, BLOCK, BLOCK), f32),
        ],
        in_specs=[SMEM] + [VMEM] * 10,
        out_specs=[VMEM] * 2,
        scratch_shapes=[
            pltpu.VMEM((BLOCK, STORED + BLOCK), f32),
            pltpu.VMEM(product.shape, f32),
        ],
        compiler_params=pltpu.CompilerParams(vmem_limit_bytes=24 << 20),
        cost_estimate=pl.CostEstimate(flops=2 << 30, bytes_accessed=6 << 20, transcendentals=0),
        name="second_block",
    )(place, *mine, others, inner, product, stored, fresh, upper)


def local(hessian, neighbours, counts, basis_vectors):
    me = lax.axis_index("blk")
    dom = lax.axis_index("dom")
    place = jnp.stack([me, dom % N_CORE]).astype(jnp.int32)
    unit_z, unit_x = N_CORE, N_CORE * N_Z
    tiles, listed = neighbours.shape
    scale = 1.0 / (basis_vectors.shape[1] * N_DOM)

    offset = (neighbours // tiles - dom + 2) % N_DOM
    odd = dom % N_CORE == 1
    offset = jnp.where(odd & (offset == 1), 3, jnp.where(odd & (offset == 3), 5, offset))
    slots = offset * tiles + neighbours % tiles
    live = jnp.arange(listed)[None, :] < counts[:, None]
    slots = jnp.where(live, slots, SPAN * tiles).reshape(-1)

    low, top = basis_vectors[:BLOCK], basis_vectors[BLOCK:]
    up_top, down_top = along(top, "blk", 1), along(top, "blk", -1)
    across = lax.ppermute(top, "blk", [(3, 1)])
    current = jnp.where(me < 2, jnp.where(me == 0, up_top, across), jnp.where(me == 2, down_top, top))
    current, low, slots, place = lax.optimization_barrier((current, low, slots, place))
    up_low, down_low = along(low, "blk", 1), along(low, "blk", -1)

    product = neighbour_product(current, hessian, slots)
    from_low, from_top, product = lax.optimization_barrier((up_low, down_top, product))
    far = [along(from_low, "blk", 1), along(from_top, "blk", -1)]
    pieces = first_sums(place, [low, top, down_low, down_top, up_low, up_top], product)
    pieces = lax.all_to_all(pieces, "dom", 0, 0, tiled=True)
    total, *far = lax.optimization_barrier((jnp.sum(pieces, axis=0), *far))
    stored = ordered(place, [low, top, down_low, down_top, *far, up_low, up_top])
    spread = lax.all_to_all(
        jnp.broadcast_to(total[None], pieces.shape), "dom", 0, 0, tiled=True
    )
    spread = over_blk(spread[: N_DOM // 2], spread[N_DOM // 2 :])
    first, upper, inner = first_block(place, spread, product, stored, scale)

    product = neighbour_product(first, hessian, slots)
    kept, sent = second_sums(place, product, first, stored)
    part = kept + flipped(sent, 1)
    part = summed(part, unit_x, (1, 2, 3))
    part = summed(part, unit_z, (1,))
    part = summed(part, unit_z, (2, 4, 6))
    mine = [part] + [along(part, "blk", -k) for k in (1, 2, 3)]
    others = flipped(jnp.stack(mine), 1)
    return second_block(place, mine, others, inner, product, stored, first, upper, scale)


def solution(mesh):
    placed = (P("dom", None, None, None), P("dom", None), P("dom"), P("blk", "dom"))
    return jax.shard_map(
        local, mesh=mesh, in_specs=placed, out_specs=(P(None, "blk", "dom"), P()), check_vma=False
    )
```

```python
import functools

import jax
import jax.numpy as jnp
from jax import lax
from jax.experimental import pallas as pl
from jax.experimental.pallas import tpu as pltpu
from jax.sharding import PartitionSpec as P

BLOCK = 64
STORED = 512
N_DOM = 64
N_X, N_Z, N_CORE = 4, 8, 2
N_BLK = 4
OWN = BLOCK // N_BLK
TILES = 57
SPAN = 5
FETCH_LIMIT = 40
PRODUCT_LIMIT = 20


bf16 = jnp.bfloat16
f32 = jnp.float32


def split(value):
    top = value.astype(bf16)
    return top, (value - top.astype(f32)).astype(bf16)


def product_of(a, b, side):
    rows = a.shape[0]
    dims = (((1,), (side,)), ((), ()))
    a_top, a_rest = split(a)
    b_top, b_rest = split(b)
    both = lax.dot_general(
        jnp.concatenate([a_top, a_rest], axis=0), b_top, dims, preferred_element_type=f32
    )
    small = lax.dot_general(a_top, b_rest, dims, preferred_element_type=f32)
    return both[:rows] + (both[rows:] + small)


def exactly(a, b, side):
    return lax.dot_general(
        a,
        b,
        (((1,), (side,)), ((), ())),
        precision=lax.Precision.HIGHEST,
        preferred_element_type=f32,
    )


def closely(a, b):
    rows = a.shape[0]
    dims = (((1,), (0,)), ((), ()))
    a_top, a_mid = split(a)
    a_low = (a - a_top.astype(f32) - a_mid.astype(f32)).astype(bf16)
    b_top, b_mid = split(b)
    b_low = (b - b_top.astype(f32) - b_mid.astype(f32)).astype(bf16)
    parts = jnp.concatenate([a_top, a_mid, a_low], axis=0)
    one = lax.dot_general(parts, b_top, dims, preferred_element_type=f32)
    two = lax.dot_general(parts[: 2 * rows], b_mid, dims, preferred_element_type=f32)
    three = lax.dot_general(a_top, b_low, dims, preferred_element_type=f32)
    small = one[2 * rows :] + two[rows:] + three
    return one[:rows] + (one[rows : 2 * rows] + two[:rows] + small)


def nt(a, b):
    return product_of(a, b, 1)


def flipped(value, mask):
    return lax.ppermute(value, "dom", [(i, i ^ mask) for i in range(N_DOM)])


def along(value, axis, by):
    peers = lax.axis_size(axis)
    return lax.ppermute(value, axis, [(i, (i + by) % peers) for i in range(peers)])


def tree_sum(parts):
    while len(parts) > 1:
        parts = [parts[i] + parts[i + 1] for i in range(0, len(parts), 2)]
    return parts[0]


def summed(value, unit, steps):
    return tree_sum([value] + [flipped(value, unit * k) for k in steps])


VMEM = pl.BlockSpec(memory_space=pltpu.VMEM)
SMEM = pl.BlockSpec(memory_space=pltpu.SMEM)


def over_blk(low, top):
    up_low, down_top = along(low, "blk", 1), along(top, "blk", -1)
    up_top, down_low = along(top, "blk", 1), along(low, "blk", -1)
    far_low, far_top = along(up_low, "blk", 1), along(down_top, "blk", -1)
    return [low, top, down_low, down_top, far_low, far_top, up_low, up_top]


def fetch_kernel(hess_ref, after_ref, out_ref, sems):
    tiles = hess_ref.shape[0]
    copies = [pltpu.make_async_copy(hess_ref.at[t], out_ref.at[t], sems.at[t]) for t in range(tiles)]
    for copy in copies:
        copy.start()
    for copy in copies:
        copy.wait()


def fetched(hessian, after):
    return pl.pallas_call(
        fetch_kernel,
        out_shape=pltpu.VMEM(hessian.shape, f32),
        in_specs=[pl.BlockSpec(memory_space=pltpu.HBM), VMEM],
        out_specs=VMEM,
        scratch_shapes=[pltpu.SemaphoreType.DMA((hessian.shape[0],))],
        compiler_params=pltpu.CompilerParams(vmem_limit_bytes=FETCH_LIMIT << 20),
        cost_estimate=pl.CostEstimate(flops=0, bytes_accessed=20 << 20, transcendentals=0),
        name="fetch",
    )(hessian, after)


def product_kernel(slots_ref, hess_ref, *refs):
    pieces, out_ref, parts, result = refs[:SPAN], *refs[SPAN:]
    tiles, listed, rows = hess_ref.shape[:3]
    for p in range(SPAN):
        values = pieces[p][...]
        for q in range(tiles):
            parts[tiles * p + q] = jnp.concatenate(
                split(values[:, rows * q : rows * (q + 1)]), axis=0
            )
    parts[SPAN * tiles] = jnp.zeros((2 * BLOCK, rows), bf16)
    dims = (((1,), (1,)), ((), ()))

    def tile(t, carry):
        first = jnp.zeros((2 * BLOCK, rows), f32)
        second = jnp.zeros((BLOCK, rows), f32)
        for k in range(listed):
            x = parts[slots_ref[t * listed + k]]
            top, rest = split(hess_ref[t, k])
            first = first + lax.dot_general(x, top, dims, preferred_element_type=f32)
            second = second + lax.dot_general(x[:BLOCK], rest, dims, preferred_element_type=f32)
        result[t] = first[:BLOCK] + (first[BLOCK:] + second)
        return carry

    lax.fori_loop(0, tiles, tile, 0)
    out_ref[...] = jnp.concatenate([result[t] for t in range(tiles)], axis=1)


def neighbour_product(block, hessian, slots):
    tiles, rows = hessian.shape[0], hessian.shape[2]
    pieces = [
        block if offset == 0 else along(block, "dom", offset) for offset in (2, 1, 0, -1, -2)
    ]
    held = fetched(hessian, block)
    return pl.pallas_call(
        product_kernel,
        out_shape=jax.ShapeDtypeStruct(block.shape, f32),
        grid_spec=pltpu.PrefetchScalarGridSpec(
            num_scalar_prefetch=1,
            grid=(),
            in_specs=[VMEM] * (1 + SPAN),
            out_specs=VMEM,
            scratch_shapes=[
                pltpu.VMEM((SPAN * tiles + 1, 2 * BLOCK, rows), bf16),
                pltpu.VMEM((tiles, BLOCK, rows), f32),
            ],
        ),
        compiler_params=pltpu.CompilerParams(vmem_limit_bytes=PRODUCT_LIMIT << 20),
        cost_estimate=pl.CostEstimate(flops=4 << 30, bytes_accessed=12 << 20, transcendentals=0),
        name="neighbour_product",
    )(slots, held, *pieces)


def eliminated(gram):
    groups = BLOCK // 8
    lanes = 2 * BLOCK
    row_ids = lax.broadcasted_iota(jnp.int32, (8, lanes), 0)
    lane_ids = lax.broadcasted_iota(jnp.int32, (8, lanes), 1)
    wide = jnp.concatenate([gram, jnp.zeros((BLOCK, BLOCK), f32)], axis=1)
    a = [
        wide[8 * g : 8 * g + 8, :] + jnp.where(lane_ids == row_ids + (8 * g + BLOCK), 1.0, 0.0)
        for g in range(groups)
    ]
    pivots = []
    for p in range(groups):
        cols = [
            [jnp.broadcast_to(a[g][:, 8 * p + c : 8 * p + c + 1], (8, lanes)) for g in range(p, groups)]
            for c in range(8)
        ]
        kept = jnp.zeros((8, lanes), f32)
        for c in range(8):
            pivot = jnp.broadcast_to(cols[c][0][c : c + 1, :], (8, lanes))
            kept = jnp.where(row_ids == c, pivot, kept)
            inverse = 1.0 / pivot
            row = jnp.broadcast_to(a[p][c : c + 1, :], (8, lanes))
            scale = [f * inverse for f in cols[c]]
            scale[0] = jnp.where(row_ids > c, scale[0], 0.0)
            for g in range(p, groups):
                a[g] = a[g] - scale[g - p] * row
            for later in range(c + 1, 8):
                level = jnp.broadcast_to(cols[later][0][c : c + 1, :], (8, lanes))
                cols[later] = [u - s * level for u, s in zip(cols[later], scale)]
        pivots.append(kept)
    return [
        jnp.where(lane_ids < row_ids + 8 * g, 0.0, a[g] * lax.rsqrt(pivots[g]))
        for g in range(groups)
    ]


def first_sums_kernel(place_ref, *refs):
    mine, after, before = [
        jnp.concatenate([refs[2 * k][...], refs[2 * k + 1][...]], axis=0) for k in range(3)
    ]
    product_ref, out_ref = refs[6], refs[7]
    for o, (a, b) in enumerate(((mine, mine), (mine, after), (before, after))):
        g = nt(a, b)
        for r in range(16):
            out_ref[16 * o + r] = g[8 * r : 8 * r + 8, :]
    c = nt(product_ref[...], mine)
    for h in range(8):
        out_ref[48 + h] = c[8 * h : 8 * h + 8, :]
    own = product_ref[pl.ds(pl.multiple_of(place_ref[0] * OWN, OWN), OWN), :]
    squares = nt(own, product_ref[...])
    out_ref[56] = jnp.concatenate([squares[:8], squares[8:]], axis=1)
    for q in range(TILES, N_DOM):
        out_ref[q] = jnp.zeros((8, 128), f32)


def first_sums(place, pieces, product):
    return pl.pallas_call(
        first_sums_kernel,
        out_shape=jax.ShapeDtypeStruct((N_DOM, 8, 128), f32),
        in_specs=[SMEM] + [VMEM] * 7,
        out_specs=VMEM,
        compiler_params=pltpu.CompilerParams(vmem_limit_bytes=20 << 20),
        cost_estimate=pl.CostEstimate(flops=2 << 30, bytes_accessed=4 << 20, transcendentals=0),
        name="first_sums",
    )(place, *pieces, product)


def ordered_kernel(place_ref, *refs):
    for k in range(8):
        row = ((place_ref[0] + k // 2) % N_BLK * 2 + k % 2) * BLOCK
        refs[8][pl.ds(pl.multiple_of(row, BLOCK), BLOCK), :] = refs[k][...]


def ordered(place, pieces):
    return pl.pallas_call(
        ordered_kernel,
        out_shape=jax.ShapeDtypeStruct((STORED, pieces[0].shape[1]), f32),
        in_specs=[SMEM] + [VMEM] * 8,
        out_specs=VMEM,
        compiler_params=pltpu.CompilerParams(vmem_limit_bytes=16 << 20),
        cost_estimate=pl.CostEstimate(flops=0, bytes_accessed=3 << 20, transcendentals=0),
        name="ordered",
    )(place, *pieces)


def finished(c, squares, inner, product, stored, fresh=None):
    d = 2.0 * c - exactly(c, inner, 0)
    f = c - exactly(d, inner, 0)
    both = jnp.concatenate(eliminated(squares - exactly(c, d, 1) - exactly(d, f, 1)), axis=0)
    upper, inverse = both[:, :BLOCK], both[:, BLOCK:]
    if fresh is not None:
        product = product - closely(d[:, :BLOCK], fresh)
        d = jnp.where(lax.broadcasted_iota(jnp.int32, d.shape, 1) < BLOCK, 0.0, d)
    return closely(inverse, product - closely(d, stored)), upper, exactly(inverse, f, 0)


def first_block_kernel(scale, place_ref, *refs):
    pieces, product_ref, stored_ref = refs[:8], refs[8], refs[9]
    block_ref, upper_ref, inner_ref, held = refs[10:]
    me = place_ref[0]
    for k in range(8):
        held[((me + k // 2) % N_BLK) * 2 + k % 2, : pieces[k].shape[0]] = pieces[k][...] * scale
    for b in range(N_BLK):
        for o, (i, j) in enumerate(((b, b), (b, b + 1), (b - 1, b + 1))):
            i, j = 128 * (i % N_BLK), 128 * (j % N_BLK)
            g = [held[2 * b + (16 * o + r) // 32, (16 * o + r) % 32] for r in range(16)]
            g = jnp.concatenate(g, axis=0)
            inner_ref[i : i + 128, j : j + 128] = g
            if o == 1:
                inner_ref[j : j + 128, i : i + 128] = g.T
    c = jnp.concatenate(
        [
            jnp.concatenate([held[2 * b + 1, 16 + h] for b in range(N_BLK)], axis=1)
            for h in range(8)
        ],
        axis=0,
    )
    squares = [held[2 * i + 1, 24] for i in range(N_BLK)]
    squares = jnp.concatenate([s[:, BLOCK * h : BLOCK * h + BLOCK] for s in squares for h in range(2)], axis=0)
    block_ref[...], upper_ref[...], crossed = finished(
        c, squares, inner_ref[...], product_ref[...], stored_ref[...]
    )
    rows = lax.broadcasted_iota(jnp.int32, crossed.shape, 0)
    lanes = lax.broadcasted_iota(jnp.int32, crossed.shape, 1)
    inner_ref[:BLOCK, :] = jnp.where(lanes < BLOCK, jnp.where(lanes == rows, 1.0, 0.0), crossed)
    inner_ref[BLOCK:, :BLOCK] = crossed.T[BLOCK:]


def first_block(place, pieces, product, stored, scale):
    shapes = [product.shape, (BLOCK, BLOCK), (STORED, STORED)]
    return pl.pallas_call(
        functools.partial(first_block_kernel, scale),
        out_shape=[jax.ShapeDtypeStruct(s, f32) for s in shapes],
        in_specs=[SMEM] + [VMEM] * 10,
        out_specs=[VMEM] * 3,
        scratch_shapes=[pltpu.VMEM((2 * N_BLK, N_DOM // 2, 8, 128), f32)],
        compiler_params=pltpu.CompilerParams(vmem_limit_bytes=24 << 20),
        cost_estimate=pl.CostEstimate(flops=2 << 30, bytes_accessed=6 << 20, transcendentals=0),
        name="first_block",
    )(place, *pieces, product, stored)


def second_sums_kernel(place_ref, product_ref, fresh_ref, stored_ref, kept_ref, sent_ref, sums):
    me, core = place_ref[0], place_ref[1]
    own = product_ref[pl.ds(pl.multiple_of(me * OWN, OWN), OWN), :]
    sums[:, :STORED] = nt(own, stored_ref[...])
    sums[:, :BLOCK] = nt(own, fresh_ref[...])
    sums[:, STORED:] = nt(own, product_ref[...])
    half = OWN // N_CORE
    kept_ref[...] = sums[pl.ds(pl.multiple_of(core * half, half), half), :]
    sent_ref[...] = sums[pl.ds(pl.multiple_of((1 - core) * half, half), half), :]


def second_sums(place, product, fresh, stored):
    return pl.pallas_call(
        second_sums_kernel,
        out_shape=[jax.ShapeDtypeStruct((OWN // N_CORE, STORED + BLOCK), f32)] * 2,
        in_specs=[SMEM] + [VMEM] * 3,
        out_specs=[VMEM] * 2,
        scratch_shapes=[pltpu.VMEM((OWN, STORED + BLOCK), f32)],
        compiler_params=pltpu.CompilerParams(vmem_limit_bytes=16 << 20),
        cost_estimate=pl.CostEstimate(flops=1 << 28, bytes_accessed=2 << 20, transcendentals=0),
        name="second_sums",
    )(place, product, fresh, stored)


def second_block_kernel(scale, place_ref, *refs):
    mine, others = refs[:4], refs[4]
    inner_ref, product_ref, stored_ref, fresh_ref, upper_ref = refs[5:10]
    blocks_ref, factors_ref, sums, whole = refs[10:]
    me, core = place_ref[0], place_ref[1]
    for k in range(N_BLK):
        row = (me + k) % N_BLK * OWN
        sums[pl.ds(pl.multiple_of(row + core * 8, 8), 8), :] = mine[k][...] * scale
        sums[pl.ds(pl.multiple_of(row + (1 - core) * 8, 8), 8), :] = others[k] * scale
    block, factors_ref[1], _ = finished(
        sums[:, :STORED],
        sums[:, STORED:],
        inner_ref[...],
        product_ref[...],
        stored_ref[...],
        fresh_ref[...],
    )
    whole[...] = block
    rows = pl.ds(pl.multiple_of(me * OWN, OWN), OWN)
    blocks_ref[0] = fresh_ref[rows, :]
    blocks_ref[1] = whole[rows, :]
    factors_ref[0] = upper_ref[...]


def second_block(place, mine, others, inner, product, stored, fresh, upper, scale):
    return pl.pallas_call(
        functools.partial(second_block_kernel, scale),
        out_shape=[
            jax.ShapeDtypeStruct((2, OWN, product.shape[1]), f32),
            jax.ShapeDtypeStruct((2, BLOCK, BLOCK), f32),
        ],
        in_specs=[SMEM] + [VMEM] * 10,
        out_specs=[VMEM] * 2,
        scratch_shapes=[
            pltpu.VMEM((BLOCK, STORED + BLOCK), f32),
            pltpu.VMEM(product.shape, f32),
        ],
        compiler_params=pltpu.CompilerParams(vmem_limit_bytes=24 << 20),
        cost_estimate=pl.CostEstimate(flops=2 << 30, bytes_accessed=6 << 20, transcendentals=0),
        name="second_block",
    )(place, *mine, others, inner, product, stored, fresh, upper)


def local(hessian, neighbours, counts, basis_vectors):
    me = lax.axis_index("blk")
    dom = lax.axis_index("dom")
    place = jnp.stack([me, dom % N_CORE]).astype(jnp.int32)
    unit_z, unit_x = N_CORE, N_CORE * N_Z
    tiles, listed = neighbours.shape
    scale = 1.0 / (basis_vectors.shape[1] * N_DOM)

    slots = (neighbours // tiles - dom + 2) % N_DOM * tiles + neighbours % tiles
    live = jnp.arange(listed)[None, :] < counts[:, None]
    slots = jnp.where(live, slots, SPAN * tiles).reshape(-1)

    low, top = basis_vectors[:BLOCK], basis_vectors[BLOCK:]
    up_top, down_top = along(top, "blk", 1), along(top, "blk", -1)
    across = lax.ppermute(top, "blk", [(3, 1)])
    current = jnp.where(me < 2, jnp.where(me == 0, up_top, across), jnp.where(me == 2, down_top, top))
    current, slots, place = lax.optimization_barrier((current, slots, place))
    up_low, down_low = along(low, "blk", 1), along(low, "blk", -1)

    product = neighbour_product(current, hessian, slots)
    from_low, from_top, product = lax.optimization_barrier((up_low, down_top, product))
    far = [along(from_low, "blk", 1), along(from_top, "blk", -1)]
    pieces = first_sums(place, [low, top, down_low, down_top, up_low, up_top], product)
    pieces = lax.all_to_all(pieces, "dom", 0, 0, tiled=True)
    total, *far = lax.optimization_barrier((jnp.sum(pieces, axis=0), *far))
    stored = ordered(place, [low, top, down_low, down_top, *far, up_low, up_top])
    spread = lax.all_to_all(
        jnp.broadcast_to(total[None], pieces.shape), "dom", 0, 0, tiled=True
    )
    spread = over_blk(spread[: N_DOM // 2], spread[N_DOM // 2 : TILES])
    first, upper, inner = first_block(place, spread, product, stored, scale)

    product = neighbour_product(first, hessian, slots)
    kept, sent = second_sums(place, product, first, stored)
    part = kept + flipped(sent, 1)
    part = summed(part, unit_x, (1, 2, 3))
    part = summed(part, unit_z, (1,))
    part = summed(part, unit_z, (2, 4, 6))
    mine = [part] + [along(part, "blk", -k) for k in (1, 2, 3)]
    others = flipped(jnp.stack(mine), 1)
    return second_block(place, mine, others, inner, product, stored, first, upper, scale)


def solution(mesh):
    placed = (P("dom", None, None, None), P("dom", None), P("dom"), P("blk", "dom"))
    return jax.shard_map(
        local, mesh=mesh, in_specs=placed, out_specs=(P(None, "blk", "dom"), P()), check_vma=False
    )
```

```python
import functools

import jax
import jax.numpy as jnp
from jax import lax
from jax.experimental import pallas as pl
from jax.experimental.pallas import tpu as pltpu
from jax.sharding import PartitionSpec as P

BLOCK = 64
STORED = 512
N_DOM = 64
N_X, N_Z, N_CORE = 4, 8, 2
N_BLK = 4
OWN = BLOCK // N_BLK
TILES = 57
SPAN = 5
FETCH_LIMIT = 40
PRODUCT_LIMIT = 20


bf16 = jnp.bfloat16
f32 = jnp.float32


def split(value):
    top = value.astype(bf16)
    return top, (value - top.astype(f32)).astype(bf16)


def nt(a, b):
    rows = a.shape[0]
    dims = (((1,), (1,)), ((), ()))
    parts = jnp.concatenate(split(a), axis=0)
    b_top, b_rest = split(b)
    one = lax.dot_general(parts, b_top, dims, preferred_element_type=f32)
    two = lax.dot_general(parts, b_rest, dims, preferred_element_type=f32)
    return one[:rows] + (one[rows:] + two[:rows] + two[rows:])


def exactly(a, b, side):
    return lax.dot_general(
        a,
        b,
        (((1,), (side,)), ((), ())),
        precision=lax.Precision.HIGHEST,
        preferred_element_type=f32,
    )


def closely(a, b):
    rows = a.shape[0]
    dims = (((1,), (0,)), ((), ()))
    a_top, a_mid = split(a)
    a_low = (a - a_top.astype(f32) - a_mid.astype(f32)).astype(bf16)
    b_top, b_mid = split(b)
    b_low = (b - b_top.astype(f32) - b_mid.astype(f32)).astype(bf16)
    parts = jnp.concatenate([a_top, a_mid, a_low], axis=0)
    one = lax.dot_general(parts, b_top, dims, preferred_element_type=f32)
    two = lax.dot_general(parts[: 2 * rows], b_mid, dims, preferred_element_type=f32)
    three = lax.dot_general(a_top, b_low, dims, preferred_element_type=f32)
    small = one[2 * rows :] + two[rows:] + three
    return one[:rows] + (one[rows : 2 * rows] + two[:rows] + small)


def flipped(value, mask):
    return lax.ppermute(value, "dom", [(i, i ^ mask) for i in range(N_DOM)])


def along(value, axis, by):
    peers = lax.axis_size(axis)
    return lax.ppermute(value, axis, [(i, (i + by) % peers) for i in range(peers)])


def tree_sum(parts):
    while len(parts) > 1:
        parts = [parts[i] + parts[i + 1] for i in range(0, len(parts), 2)]
    return parts[0]


def summed(value, unit, steps):
    got = {k: flipped(value, unit * k) for k in steps}
    return tree_sum([value] + [got[k] for k in sorted(got)])


def around(value):
    got = {k: along(value, "blk", -k) for k in (1, 3, 2)}
    return [value] + [got[k] for k in (1, 2, 3)]


VMEM = pl.BlockSpec(memory_space=pltpu.VMEM)
SMEM = pl.BlockSpec(memory_space=pltpu.SMEM)


def over_blk(low, top):
    up_low, down_top = along(low, "blk", 1), along(top, "blk", -1)
    up_top, down_low = along(top, "blk", 1), along(low, "blk", -1)
    far_low, far_top = along(up_low, "blk", 1), along(down_top, "blk", -1)
    return [low, top, down_low, down_top, far_low, far_top, up_low, up_top]


def fetch_kernel(hess_ref, after_ref, out_ref, sems):
    tiles = hess_ref.shape[0]
    copies = [pltpu.make_async_copy(hess_ref.at[t], out_ref.at[t], sems.at[t]) for t in range(tiles)]
    for copy in copies:
        copy.start()
    for copy in copies:
        copy.wait()


def fetched(hessian, after):
    return pl.pallas_call(
        fetch_kernel,
        out_shape=pltpu.VMEM(hessian.shape, f32),
        in_specs=[pl.BlockSpec(memory_space=pltpu.HBM), VMEM],
        out_specs=VMEM,
        scratch_shapes=[pltpu.SemaphoreType.DMA((hessian.shape[0],))],
        compiler_params=pltpu.CompilerParams(vmem_limit_bytes=FETCH_LIMIT << 20),
        cost_estimate=pl.CostEstimate(flops=0, bytes_accessed=20 << 20, transcendentals=0),
        name="fetch",
    )(hessian, after)


def product_kernel(slots_ref, hess_ref, *refs):
    pieces, out_ref, parts, result = refs[:SPAN], *refs[SPAN:]
    tiles, listed, rows = hess_ref.shape[:3]
    block = out_ref.shape[0]
    for p in range(SPAN):
        values = pieces[p][...]
        for q in range(tiles):
            parts[tiles * p + q] = jnp.concatenate(
                split(values[:, rows * q : rows * (q + 1)]), axis=0
            )
    parts[SPAN * tiles] = jnp.zeros((2 * block, rows), bf16)
    dims = (((1,), (1,)), ((), ()))

    def tile(t, carry):
        first = jnp.zeros((2 * block, rows), f32)
        second = jnp.zeros((block, rows), f32)
        for k in range(listed):
            x = parts[slots_ref[t * listed + k]]
            top, rest = split(hess_ref[t, k])
            first = first + lax.dot_general(x, top, dims, preferred_element_type=f32)
            second = second + lax.dot_general(x[:block], rest, dims, preferred_element_type=f32)
        result[t] = first[:block] + (first[block:] + second)
        return carry

    lax.fori_loop(0, tiles, tile, 0)
    out_ref[...] = jnp.concatenate([result[t] for t in range(tiles)], axis=1)


def neighbour_product(block, hessian, slots):
    tiles, rows = hessian.shape[0], hessian.shape[2]
    pieces = [
        block if offset == 0 else along(block, "dom", offset) for offset in (2, 1, 0, -1, -2)
    ]
    held = fetched(hessian, block)
    return pl.pallas_call(
        product_kernel,
        out_shape=jax.ShapeDtypeStruct(block.shape, f32),
        grid_spec=pltpu.PrefetchScalarGridSpec(
            num_scalar_prefetch=1,
            grid=(),
            in_specs=[VMEM] * (1 + SPAN),
            out_specs=VMEM,
            scratch_shapes=[
                pltpu.VMEM((SPAN * tiles + 1, 2 * block.shape[0], rows), bf16),
                pltpu.VMEM((tiles, block.shape[0], rows), f32),
            ],
        ),
        compiler_params=pltpu.CompilerParams(vmem_limit_bytes=PRODUCT_LIMIT << 20),
        cost_estimate=pl.CostEstimate(flops=4 << 30, bytes_accessed=12 << 20, transcendentals=0),
        name="neighbour_product",
    )(slots, held, *pieces)


def eliminated(gram):
    groups = BLOCK // 8
    lanes = 2 * BLOCK
    row_ids = lax.broadcasted_iota(jnp.int32, (8, lanes), 0)
    lane_ids = lax.broadcasted_iota(jnp.int32, (8, lanes), 1)
    wide = jnp.concatenate([gram, jnp.zeros((BLOCK, BLOCK), f32)], axis=1)
    a = [
        wide[8 * g : 8 * g + 8, :] + jnp.where(lane_ids == row_ids + (8 * g + BLOCK), 1.0, 0.0)
        for g in range(groups)
    ]
    pivots = []
    for p in range(groups):
        cols = [
            [jnp.broadcast_to(a[g][:, 8 * p + c : 8 * p + c + 1], (8, lanes)) for g in range(p, groups)]
            for c in range(8)
        ]
        kept = jnp.zeros((8, lanes), f32)
        for c in range(8):
            pivot = jnp.broadcast_to(cols[c][0][c : c + 1, :], (8, lanes))
            kept = jnp.where(row_ids == c, pivot, kept)
            inverse = 1.0 / pivot
            row = jnp.broadcast_to(a[p][c : c + 1, :], (8, lanes))
            scale = [f * inverse for f in cols[c]]
            scale[0] = jnp.where(row_ids > c, scale[0], 0.0)
            for g in range(p, groups):
                a[g] = a[g] - scale[g - p] * row
            for later in range(c + 1, 8):
                level = jnp.broadcast_to(cols[later][0][c : c + 1, :], (8, lanes))
                cols[later] = [u - s * level for u, s in zip(cols[later], scale)]
        pivots.append(kept)
    return [
        jnp.where(lane_ids < row_ids + 8 * g, 0.0, a[g] * lax.rsqrt(pivots[g]))
        for g in range(groups)
    ]


def first_sums_kernel(place_ref, *refs):
    mine, after, before, product_ref, out_ref = refs[0], refs[1], refs[2], refs[7], refs[8]
    for k in range(N_BLK):
        row = (place_ref[0] + k) % N_BLK * OWN
        product_ref[pl.ds(pl.multiple_of(row, OWN), OWN), :] = refs[3 + k][...]
    for o, (a, b) in enumerate(((mine, mine), (mine, after), (before, after))):
        g = nt(a[...], b[...])
        for r in range(16):
            out_ref[16 * o + r] = g[8 * r : 8 * r + 8, :]
    c = nt(product_ref[...], mine[...])
    for h in range(8):
        out_ref[48 + h] = c[8 * h : 8 * h + 8, :]
    squares = nt(refs[3][...], product_ref[...])
    out_ref[56] = jnp.concatenate([squares[:8], squares[8:]], axis=1)
    for q in range(TILES, N_DOM):
        out_ref[q] = jnp.zeros((8, 128), f32)


def first_sums(place, rows, products):
    return pl.pallas_call(
        first_sums_kernel,
        out_shape=[
            jax.ShapeDtypeStruct((BLOCK, products[0].shape[1]), f32),
            jax.ShapeDtypeStruct((N_DOM, 8, 128), f32),
        ],
        in_specs=[SMEM] + [VMEM] * 7,
        out_specs=[VMEM] * 2,
        compiler_params=pltpu.CompilerParams(vmem_limit_bytes=20 << 20),
        cost_estimate=pl.CostEstimate(flops=2 << 30, bytes_accessed=4 << 20, transcendentals=0),
        name="first_sums",
    )(place, *rows, *products)


def ordered_kernel(place_ref, *refs):
    rows = refs[0].shape[0]
    for k in range(N_BLK):
        row = (place_ref[0] + k) % N_BLK * rows
        refs[N_BLK][pl.ds(pl.multiple_of(row, rows), rows), :] = refs[k][...]


def ordered(place, pieces):
    return pl.pallas_call(
        ordered_kernel,
        out_shape=jax.ShapeDtypeStruct((STORED, pieces[0].shape[1]), f32),
        in_specs=[SMEM] + [VMEM] * N_BLK,
        out_specs=VMEM,
        compiler_params=pltpu.CompilerParams(vmem_limit_bytes=16 << 20),
        cost_estimate=pl.CostEstimate(flops=0, bytes_accessed=3 << 20, transcendentals=0),
        name="ordered",
    )(place, *pieces)


def finished(c, squares, inner, product, stored, fresh=None):
    d = 2.0 * c - exactly(c, inner, 0)
    f = c - exactly(d, inner, 0)
    both = jnp.concatenate(eliminated(squares - exactly(c, d, 1) - exactly(d, f, 1)), axis=0)
    upper, inverse = both[:, :BLOCK], both[:, BLOCK:]
    if fresh is not None:
        product = product - closely(d[:, :BLOCK], fresh)
        d = jnp.where(lax.broadcasted_iota(jnp.int32, d.shape, 1) < BLOCK, 0.0, d)
    return closely(inverse, product - closely(d, stored)), upper, exactly(inverse, f, 0)


def first_block_kernel(scale, place_ref, *refs):
    pieces, product_ref, stored_ref = refs[:8], refs[8], refs[9]
    block_ref, upper_ref, inner_ref, held = refs[10:]
    me = place_ref[0]
    for k in range(8):
        held[((me + k // 2) % N_BLK) * 2 + k % 2, : pieces[k].shape[0]] = pieces[k][...] * scale
    for b in range(N_BLK):
        for o, (i, j) in enumerate(((b, b), (b, b + 1), (b - 1, b + 1))):
            i, j = 128 * (i % N_BLK), 128 * (j % N_BLK)
            g = [held[2 * b + (16 * o + r) // 32, (16 * o + r) % 32] for r in range(16)]
            g = jnp.concatenate(g, axis=0)
            inner_ref[i : i + 128, j : j + 128] = g
            if o == 1:
                inner_ref[j : j + 128, i : i + 128] = g.T
    c = jnp.concatenate(
        [
            jnp.concatenate([held[2 * b + 1, 16 + h] for b in range(N_BLK)], axis=1)
            for h in range(8)
        ],
        axis=0,
    )
    squares = [held[2 * i + 1, 24] for i in range(N_BLK)]
    squares = jnp.concatenate([s[:, BLOCK * h : BLOCK * h + BLOCK] for s in squares for h in range(2)], axis=0)
    block_ref[...], upper_ref[...], crossed = finished(
        c, squares, inner_ref[...], product_ref[...], stored_ref[...]
    )
    rows = lax.broadcasted_iota(jnp.int32, crossed.shape, 0)
    lanes = lax.broadcasted_iota(jnp.int32, crossed.shape, 1)
    inner_ref[:BLOCK, :] = jnp.where(lanes < BLOCK, jnp.where(lanes == rows, 1.0, 0.0), crossed)
    inner_ref[BLOCK:, :BLOCK] = crossed.T[BLOCK:]


def first_block(place, pieces, product, stored, scale):
    shapes = [product.shape, (BLOCK, BLOCK), (STORED, STORED)]
    return pl.pallas_call(
        functools.partial(first_block_kernel, scale),
        out_shape=[jax.ShapeDtypeStruct(s, f32) for s in shapes],
        in_specs=[SMEM] + [VMEM] * 10,
        out_specs=[VMEM] * 3,
        scratch_shapes=[pltpu.VMEM((2 * N_BLK, N_DOM // 2, 8, 128), f32)],
        compiler_params=pltpu.CompilerParams(vmem_limit_bytes=24 << 20),
        cost_estimate=pl.CostEstimate(flops=2 << 30, bytes_accessed=6 << 20, transcendentals=0),
        name="first_block",
    )(place, *pieces, product, stored)


def second_sums_kernel(place_ref, product_ref, fresh_ref, stored_ref, kept_ref, sent_ref, sums):
    me, core = place_ref[0], place_ref[1]
    own = product_ref[pl.ds(pl.multiple_of(me * OWN, OWN), OWN), :]
    sums[:, :STORED] = nt(own, stored_ref[...])
    sums[:, :BLOCK] = nt(own, fresh_ref[...])
    sums[:, STORED:] = nt(own, product_ref[...])
    half = OWN // N_CORE
    kept_ref[...] = sums[pl.ds(pl.multiple_of(core * half, half), half), :]
    sent_ref[...] = sums[pl.ds(pl.multiple_of((1 - core) * half, half), half), :]


def second_sums(place, product, fresh, stored):
    return pl.pallas_call(
        second_sums_kernel,
        out_shape=[jax.ShapeDtypeStruct((OWN // N_CORE, STORED + BLOCK), f32)] * 2,
        in_specs=[SMEM] + [VMEM] * 3,
        out_specs=[VMEM] * 2,
        scratch_shapes=[pltpu.VMEM((OWN, STORED + BLOCK), f32)],
        compiler_params=pltpu.CompilerParams(vmem_limit_bytes=16 << 20),
        cost_estimate=pl.CostEstimate(flops=1 << 28, bytes_accessed=2 << 20, transcendentals=0),
        name="second_sums",
    )(place, product, fresh, stored)


def second_block_kernel(scale, place_ref, *refs):
    mine, others = refs[:4], refs[4]
    inner_ref, product_ref, stored_ref, fresh_ref, upper_ref = refs[5:10]
    blocks_ref, factors_ref, sums, whole = refs[10:]
    me, core = place_ref[0], place_ref[1]
    for k in range(N_BLK):
        row = (me + k) % N_BLK * OWN
        sums[pl.ds(pl.multiple_of(row + core * 8, 8), 8), :] = mine[k][...] * scale
        sums[pl.ds(pl.multiple_of(row + (1 - core) * 8, 8), 8), :] = others[k] * scale
    block, factors_ref[1], _ = finished(
        sums[:, :STORED],
        sums[:, STORED:],
        inner_ref[...],
        product_ref[...],
        stored_ref[...],
        fresh_ref[...],
    )
    whole[...] = block
    rows = pl.ds(pl.multiple_of(me * OWN, OWN), OWN)
    blocks_ref[0] = fresh_ref[rows, :]
    blocks_ref[1] = whole[rows, :]
    factors_ref[0] = upper_ref[...]


def second_block(place, mine, others, inner, product, stored, fresh, upper, scale):
    return pl.pallas_call(
        functools.partial(second_block_kernel, scale),
        out_shape=[
            jax.ShapeDtypeStruct((2, OWN, product.shape[1]), f32),
            jax.ShapeDtypeStruct((2, BLOCK, BLOCK), f32),
        ],
        in_specs=[SMEM] + [VMEM] * 10,
        out_specs=[VMEM] * 2,
        scratch_shapes=[
            pltpu.VMEM((BLOCK, STORED + BLOCK), f32),
            pltpu.VMEM(product.shape, f32),
        ],
        compiler_params=pltpu.CompilerParams(vmem_limit_bytes=24 << 20),
        cost_estimate=pl.CostEstimate(flops=2 << 30, bytes_accessed=6 << 20, transcendentals=0),
        name="second_block",
    )(place, *mine, others, inner, product, stored, fresh, upper)


def local(hessian, neighbours, counts, basis_vectors):
    me = lax.axis_index("blk")
    dom = lax.axis_index("dom")
    place = jnp.stack([me, dom % N_CORE]).astype(jnp.int32)
    unit_z, unit_x = N_CORE, N_CORE * N_Z
    tiles, listed = neighbours.shape
    scale = 1.0 / (basis_vectors.shape[1] * N_DOM)

    slots = (neighbours // tiles - dom + 2) % N_DOM * tiles + neighbours % tiles
    live = jnp.arange(listed)[None, :] < counts[:, None]
    slots = jnp.where(live, slots, SPAN * tiles).reshape(-1)

    arrived = [
        lax.ppermute(basis_vectors[BLOCK + OWN * k : BLOCK + OWN * (k + 1)], "blk", [(N_BLK - 1, k)])
        for k in (0, 2, 1)
    ]
    current = jnp.where(
        me == N_BLK - 1, basis_vectors[-OWN:], arrived[0] + arrived[1] + arrived[2]
    )
    current, slots, place, rows = lax.optimization_barrier((current, slots, place, basis_vectors))
    before, after = along(rows, "blk", 1), along(rows, "blk", -1)

    own = neighbour_product(current, hessian, slots)
    products = around(own)
    onward, *products = lax.optimization_barrier((before, *products))
    far = along(onward, "blk", 1)
    product, pieces = first_sums(place, [rows, after, before], products)
    pieces = lax.all_to_all(pieces, "dom", 0, 0, tiled=True)
    total, far = lax.optimization_barrier((jnp.sum(pieces, axis=0), far))
    stored = ordered(place, [rows, after, far, before])
    spread = lax.all_to_all(
        jnp.broadcast_to(total[None], pieces.shape), "dom", 0, 0, tiled=True
    )
    spread = over_blk(spread[: N_DOM // 2], spread[N_DOM // 2 : TILES])
    first, upper, inner = first_block(place, spread, product, stored, scale)

    product = neighbour_product(first, hessian, slots)
    kept, sent = second_sums(place, product, first, stored)
    part = kept + flipped(sent, 1)
    part = summed(part, unit_x, (1, 3, 2))
    part = summed(part, unit_z, (1,))
    part = summed(part, unit_z, (2, 6, 4))
    mine = around(part)
    others = flipped(jnp.stack(mine), 1)
    return second_block(place, mine, others, inner, product, stored, first, upper, scale)


def solution(mesh):
    placed = (P("dom", None, None, None), P("dom", None), P("dom"), P("blk", "dom"))
    return jax.shard_map(
        local, mesh=mesh, in_specs=placed, out_specs=(P(None, "blk", "dom"), P()), check_vma=False
    )
```

```python
import functools

import jax
import jax.numpy as jnp
from jax import lax
from jax.experimental import pallas as pl
from jax.experimental.pallas import tpu as pltpu
from jax.sharding import PartitionSpec as P

BLOCK = 64
STORED = 512
N_DOM = 64
N_X, N_Z, N_CORE = 4, 8, 2
N_BLK = 4
OWN = BLOCK // N_BLK
TILES = 57
SPAN = 5
FETCH_LIMIT = 40
PRODUCT_LIMIT = 20


bf16 = jnp.bfloat16
f32 = jnp.float32


def split(value):
    top = value.astype(bf16)
    return top, (value - top.astype(f32)).astype(bf16)


def nt(a, b):
    rows = a.shape[0]
    dims = (((1,), (1,)), ((), ()))
    parts = jnp.concatenate(split(a), axis=0)
    b_top, b_rest = split(b)
    one = lax.dot_general(parts, b_top, dims, preferred_element_type=f32)
    two = lax.dot_general(parts, b_rest, dims, preferred_element_type=f32)
    return one[:rows] + (one[rows:] + two[:rows] + two[rows:])


def exactly(a, b, side):
    return lax.dot_general(
        a,
        b,
        (((1,), (side,)), ((), ())),
        precision=lax.Precision.HIGHEST,
        preferred_element_type=f32,
    )


def closely(a, b):
    rows = a.shape[0]
    dims = (((1,), (0,)), ((), ()))
    a_top, a_mid = split(a)
    a_low = (a - a_top.astype(f32) - a_mid.astype(f32)).astype(bf16)
    b_top, b_mid = split(b)
    b_low = (b - b_top.astype(f32) - b_mid.astype(f32)).astype(bf16)
    parts = jnp.concatenate([a_top, a_mid, a_low], axis=0)
    one = lax.dot_general(parts, b_top, dims, preferred_element_type=f32)
    two = lax.dot_general(parts[: 2 * rows], b_mid, dims, preferred_element_type=f32)
    three = lax.dot_general(a_top, b_low, dims, preferred_element_type=f32)
    small = one[2 * rows :] + two[rows:] + three
    return one[:rows] + (one[rows : 2 * rows] + two[:rows] + small)


def flipped(value, mask):
    return lax.ppermute(value, "dom", [(i, i ^ mask) for i in range(N_DOM)])


def along(value, axis, by):
    peers = lax.axis_size(axis)
    return lax.ppermute(value, axis, [(i, (i + by) % peers) for i in range(peers)])


def tree_sum(parts):
    while len(parts) > 1:
        parts = [parts[i] + parts[i + 1] for i in range(0, len(parts), 2)]
    return parts[0]


def summed(value, unit, steps):
    return tree_sum([value] + [flipped(value, unit * k) for k in steps])


VMEM = pl.BlockSpec(memory_space=pltpu.VMEM)
SMEM = pl.BlockSpec(memory_space=pltpu.SMEM)


def over_blk(low, top):
    up_low, down_top = along(low, "blk", 1), along(top, "blk", -1)
    up_top, down_low = along(top, "blk", 1), along(low, "blk", -1)
    far_low, far_top = along(up_low, "blk", 1), along(down_top, "blk", -1)
    return [low, top, down_low, down_top, far_low, far_top, up_low, up_top]


def fetch_kernel(hess_ref, after_ref, out_ref, sems):
    tiles = hess_ref.shape[0]
    copies = [pltpu.make_async_copy(hess_ref.at[t], out_ref.at[t], sems.at[t]) for t in range(tiles)]
    for copy in copies:
        copy.start()
    for copy in copies:
        copy.wait()


def fetched(hessian, after):
    return pl.pallas_call(
        fetch_kernel,
        out_shape=pltpu.VMEM(hessian.shape, f32),
        in_specs=[pl.BlockSpec(memory_space=pltpu.HBM), VMEM],
        out_specs=VMEM,
        scratch_shapes=[pltpu.SemaphoreType.DMA((hessian.shape[0],))],
        compiler_params=pltpu.CompilerParams(vmem_limit_bytes=FETCH_LIMIT << 20),
        cost_estimate=pl.CostEstimate(flops=0, bytes_accessed=20 << 20, transcendentals=0),
        name="fetch",
    )(hessian, after)


def product_kernel(slots_ref, hess_ref, *refs):
    pieces, out_ref, parts, result = refs[:SPAN], *refs[SPAN:]
    tiles, listed, rows = hess_ref.shape[:3]
    for p in range(SPAN):
        values = pieces[p][...]
        for q in range(tiles):
            parts[tiles * p + q] = jnp.concatenate(
                split(values[:, rows * q : rows * (q + 1)]), axis=0
            )
    parts[SPAN * tiles] = jnp.zeros((2 * BLOCK, rows), bf16)
    dims = (((1,), (1,)), ((), ()))

    def tile(t, carry):
        first = jnp.zeros((2 * BLOCK, rows), f32)
        second = jnp.zeros((BLOCK, rows), f32)
        for k in range(listed):
            x = parts[slots_ref[t * listed + k]]
            top, rest = split(hess_ref[t, k])
            first = first + lax.dot_general(x, top, dims, preferred_element_type=f32)
            second = second + lax.dot_general(x[:BLOCK], rest, dims, preferred_element_type=f32)
        result[t] = first[:BLOCK] + (first[BLOCK:] + second)
        return carry

    lax.fori_loop(0, tiles, tile, 0)
    out_ref[...] = jnp.concatenate([result[t] for t in range(tiles)], axis=1)


def neighbour_product(block, hessian, slots):
    tiles, rows = hessian.shape[0], hessian.shape[2]
    pieces = [block] + [along(block, "dom", offset) for offset in (1, -1, 2, -2)]
    held = fetched(hessian, block)
    return pl.pallas_call(
        product_kernel,
        out_shape=jax.ShapeDtypeStruct(block.shape, f32),
        grid_spec=pltpu.PrefetchScalarGridSpec(
            num_scalar_prefetch=1,
            grid=(),
            in_specs=[VMEM] * (1 + SPAN),
            out_specs=VMEM,
            scratch_shapes=[
                pltpu.VMEM((SPAN * tiles + 1, 2 * BLOCK, rows), bf16),
                pltpu.VMEM((tiles, BLOCK, rows), f32),
            ],
        ),
        compiler_params=pltpu.CompilerParams(vmem_limit_bytes=PRODUCT_LIMIT << 20),
        cost_estimate=pl.CostEstimate(flops=4 << 30, bytes_accessed=12 << 20, transcendentals=0),
        name="neighbour_product",
    )(slots, held, *pieces)


def eliminated(gram):
    groups = BLOCK // 8
    lanes = 2 * BLOCK
    row_ids = lax.broadcasted_iota(jnp.int32, (8, lanes), 0)
    lane_ids = lax.broadcasted_iota(jnp.int32, (8, lanes), 1)
    wide = jnp.concatenate([gram, jnp.zeros((BLOCK, BLOCK), f32)], axis=1)
    a = [
        wide[8 * g : 8 * g + 8, :] + jnp.where(lane_ids == row_ids + (8 * g + BLOCK), 1.0, 0.0)
        for g in range(groups)
    ]
    pivots = []
    for p in range(groups):
        cols = [
            [jnp.broadcast_to(a[g][:, 8 * p + c : 8 * p + c + 1], (8, lanes)) for g in range(p, groups)]
            for c in range(8)
        ]
        kept = jnp.zeros((8, lanes), f32)
        for c in range(8):
            pivot = jnp.broadcast_to(cols[c][0][c : c + 1, :], (8, lanes))
            kept = jnp.where(row_ids == c, pivot, kept)
            inverse = 1.0 / pivot
            row = jnp.broadcast_to(a[p][c : c + 1, :], (8, lanes))
            scale = [f * inverse for f in cols[c]]
            scale[0] = jnp.where(row_ids > c, scale[0], 0.0)
            for g in range(p, groups):
                a[g] = a[g] - scale[g - p] * row
            for later in range(c + 1, 8):
                level = jnp.broadcast_to(cols[later][0][c : c + 1, :], (8, lanes))
                cols[later] = [u - s * level for u, s in zip(cols[later], scale)]
        pivots.append(kept)
    return [
        jnp.where(lane_ids < row_ids + 8 * g, 0.0, a[g] * lax.rsqrt(pivots[g]))
        for g in range(groups)
    ]


def chosen_kernel(place_ref, *refs):
    for k in range(N_BLK):

        @pl.when(place_ref[0] == k)
        def _(k=k):
            refs[N_BLK][...] = refs[k][...]


def chosen(place, options):
    return pl.pallas_call(
        chosen_kernel,
        out_shape=jax.ShapeDtypeStruct(options[0].shape, f32),
        in_specs=[SMEM] + [VMEM] * N_BLK,
        out_specs=VMEM,
        compiler_params=pltpu.CompilerParams(vmem_limit_bytes=8 << 20),
        cost_estimate=pl.CostEstimate(flops=0, bytes_accessed=1 << 19, transcendentals=0),
        name="chosen",
    )(place, *options)


def first_sums_kernel(place_ref, *refs):
    mine, after, before = [
        jnp.concatenate([refs[2 * k][...], refs[2 * k + 1][...]], axis=0) for k in range(3)
    ]
    product_ref, out_ref = refs[6], refs[7]
    for o, (a, b) in enumerate(((mine, mine), (mine, after), (before, after))):
        g = nt(a, b)
        for r in range(16):
            out_ref[16 * o + r] = g[8 * r : 8 * r + 8, :]
    c = nt(product_ref[...], mine)
    for h in range(8):
        out_ref[48 + h] = c[8 * h : 8 * h + 8, :]
    own = product_ref[pl.ds(pl.multiple_of(place_ref[0] * OWN, OWN), OWN), :]
    squares = nt(own, product_ref[...])
    out_ref[56] = jnp.concatenate([squares[:8], squares[8:]], axis=1)
    for q in range(TILES, N_DOM):
        out_ref[q] = jnp.zeros((8, 128), f32)


def first_sums(place, pieces, product):
    return pl.pallas_call(
        first_sums_kernel,
        out_shape=jax.ShapeDtypeStruct((N_DOM, 8, 128), f32),
        in_specs=[SMEM] + [VMEM] * 7,
        out_specs=VMEM,
        compiler_params=pltpu.CompilerParams(vmem_limit_bytes=20 << 20),
        cost_estimate=pl.CostEstimate(flops=2 << 30, bytes_accessed=4 << 20, transcendentals=0),
        name="first_sums",
    )(place, *pieces, product)


def ordered_kernel(place_ref, *refs):
    for k in range(8):
        row = ((place_ref[0] + k // 2) % N_BLK * 2 + k % 2) * BLOCK
        refs[8][pl.ds(pl.multiple_of(row, BLOCK), BLOCK), :] = refs[k][...]


def ordered(place, pieces):
    return pl.pallas_call(
        ordered_kernel,
        out_shape=jax.ShapeDtypeStruct((STORED, pieces[0].shape[1]), f32),
        in_specs=[SMEM] + [VMEM] * 8,
        out_specs=VMEM,
        compiler_params=pltpu.CompilerParams(vmem_limit_bytes=16 << 20),
        cost_estimate=pl.CostEstimate(flops=0, bytes_accessed=3 << 20, transcendentals=0),
        name="ordered",
    )(place, *pieces)


def finished(c, squares, inner, product, stored, fresh=None):
    d = 2.0 * c - exactly(c, inner, 0)
    f = c - exactly(d, inner, 0)
    both = jnp.concatenate(eliminated(squares - exactly(c, d, 1) - exactly(d, f, 1)), axis=0)
    upper, inverse = both[:, :BLOCK], both[:, BLOCK:]
    if fresh is not None:
        product = product - closely(d[:, :BLOCK], fresh)
        d = jnp.where(lax.broadcasted_iota(jnp.int32, d.shape, 1) < BLOCK, 0.0, d)
    return closely(inverse, product - closely(d, stored)), upper, exactly(inverse, f, 0)


def first_block_kernel(scale, place_ref, *refs):
    pieces, product_ref, stored_ref = refs[:8], refs[8], refs[9]
    block_ref, upper_ref, inner_ref, held = refs[10:]
    me = place_ref[0]
    for k in range(8):
        held[((me + k // 2) % N_BLK) * 2 + k % 2, : pieces[k].shape[0]] = pieces[k][...] * scale
    for b in range(N_BLK):
        for o, (i, j) in enumerate(((b, b), (b, b + 1), (b - 1, b + 1))):
            i, j = 128 * (i % N_BLK), 128 * (j % N_BLK)
            g = [held[2 * b + (16 * o + r) // 32, (16 * o + r) % 32] for r in range(16)]
            g = jnp.concatenate(g, axis=0)
            inner_ref[i : i + 128, j : j + 128] = g
            if o == 1:
                inner_ref[j : j + 128, i : i + 128] = g.T
    c = jnp.concatenate(
        [
            jnp.concatenate([held[2 * b + 1, 16 + h] for b in range(N_BLK)], axis=1)
            for h in range(8)
        ],
        axis=0,
    )
    squares = [held[2 * i + 1, 24] for i in range(N_BLK)]
    squares = jnp.concatenate([s[:, BLOCK * h : BLOCK * h + BLOCK] for s in squares for h in range(2)], axis=0)
    block_ref[...], upper_ref[...], crossed = finished(
        c, squares, inner_ref[...], product_ref[...], stored_ref[...]
    )
    rows = lax.broadcasted_iota(jnp.int32, crossed.shape, 0)
    lanes = lax.broadcasted_iota(jnp.int32, crossed.shape, 1)
    inner_ref[:BLOCK, :] = jnp.where(lanes < BLOCK, jnp.where(lanes == rows, 1.0, 0.0), crossed)
    inner_ref[BLOCK:, :BLOCK] = crossed.T[BLOCK:]


def first_block(place, pieces, product, stored, scale):
    shapes = [product.shape, (BLOCK, BLOCK), (STORED, STORED)]
    return pl.pallas_call(
        functools.partial(first_block_kernel, scale),
        out_shape=[jax.ShapeDtypeStruct(s, f32) for s in shapes],
        in_specs=[SMEM] + [VMEM] * 10,
        out_specs=[VMEM] * 3,
        scratch_shapes=[pltpu.VMEM((2 * N_BLK, N_DOM // 2, 8, 128), f32)],
        compiler_params=pltpu.CompilerParams(vmem_limit_bytes=24 << 20),
        cost_estimate=pl.CostEstimate(flops=2 << 30, bytes_accessed=6 << 20, transcendentals=0),
        name="first_block",
    )(place, *pieces, product, stored)


def second_sums_kernel(place_ref, product_ref, fresh_ref, stored_ref, kept_ref, sent_ref, sums):
    me, core = place_ref[0], place_ref[1]
    own = product_ref[pl.ds(pl.multiple_of(me * OWN, OWN), OWN), :]
    sums[:, :STORED] = nt(own, stored_ref[...])
    sums[:, :BLOCK] = nt(own, fresh_ref[...])
    sums[:, STORED:] = nt(own, product_ref[...])
    half = OWN // N_CORE
    kept_ref[...] = sums[pl.ds(pl.multiple_of(core * half, half), half), :]
    sent_ref[...] = sums[pl.ds(pl.multiple_of((1 - core) * half, half), half), :]


def second_sums(place, product, fresh, stored):
    return pl.pallas_call(
        second_sums_kernel,
        out_shape=[jax.ShapeDtypeStruct((OWN // N_CORE, STORED + BLOCK), f32)] * 2,
        in_specs=[SMEM] + [VMEM] * 3,
        out_specs=[VMEM] * 2,
        scratch_shapes=[pltpu.VMEM((OWN, STORED + BLOCK), f32)],
        compiler_params=pltpu.CompilerParams(vmem_limit_bytes=16 << 20),
        cost_estimate=pl.CostEstimate(flops=1 << 28, bytes_accessed=2 << 20, transcendentals=0),
        name="second_sums",
    )(place, product, fresh, stored)


def second_block_kernel(scale, place_ref, *refs):
    mine, others = refs[:4], refs[4]
    inner_ref, product_ref, stored_ref, fresh_ref, upper_ref = refs[5:10]
    blocks_ref, factors_ref, sums, whole = refs[10:]
    me, core = place_ref[0], place_ref[1]
    for k in range(N_BLK):
        row = (me + k) % N_BLK * OWN
        sums[pl.ds(pl.multiple_of(row + core * 8, 8), 8), :] = mine[k][...] * scale
        sums[pl.ds(pl.multiple_of(row + (1 - core) * 8, 8), 8), :] = others[k] * scale
    block, factors_ref[1], _ = finished(
        sums[:, :STORED],
        sums[:, STORED:],
        inner_ref[...],
        product_ref[...],
        stored_ref[...],
        fresh_ref[...],
    )
    whole[...] = block
    rows = pl.ds(pl.multiple_of(me * OWN, OWN), OWN)
    blocks_ref[0] = fresh_ref[rows, :]
    blocks_ref[1] = whole[rows, :]
    factors_ref[0] = upper_ref[...]


def second_block(place, mine, others, inner, product, stored, fresh, upper, scale):
    return pl.pallas_call(
        functools.partial(second_block_kernel, scale),
        out_shape=[
            jax.ShapeDtypeStruct((2, OWN, product.shape[1]), f32),
            jax.ShapeDtypeStruct((2, BLOCK, BLOCK), f32),
        ],
        in_specs=[SMEM] + [VMEM] * 10,
        out_specs=[VMEM] * 2,
        scratch_shapes=[
            pltpu.VMEM((BLOCK, STORED + BLOCK), f32),
            pltpu.VMEM(product.shape, f32),
        ],
        compiler_params=pltpu.CompilerParams(vmem_limit_bytes=24 << 20),
        cost_estimate=pl.CostEstimate(flops=2 << 30, bytes_accessed=6 << 20, transcendentals=0),
        name="second_block",
    )(place, *mine, others, inner, product, stored, fresh, upper)


def local(hessian, neighbours, counts, basis_vectors):
    me = lax.axis_index("blk")
    dom = lax.axis_index("dom")
    place = jnp.stack([me, dom % N_CORE]).astype(jnp.int32)
    unit_z, unit_x = N_CORE, N_CORE * N_Z
    tiles, listed = neighbours.shape
    scale = 1.0 / (basis_vectors.shape[1] * N_DOM)

    slots = (neighbours // tiles - dom + 2) % N_DOM
    slots = jnp.where(
        slots < 2, 3 - 2 * slots, jnp.where(slots == 2, 0, jnp.where(slots == 3, 2, 4))
    )
    slots = slots * tiles + neighbours % tiles
    live = jnp.arange(listed)[None, :] < counts[:, None]
    slots = jnp.where(live, slots, SPAN * tiles).reshape(-1)

    low, top = lax.optimization_barrier((basis_vectors[:BLOCK], basis_vectors[BLOCK:]))
    up_top, down_top = along(top, "blk", 1), along(top, "blk", -1)
    across = lax.ppermute(top, "blk", [(3, 1)])
    current = chosen(place, [up_top, across, down_top, top])
    current, slots, low = lax.optimization_barrier((current, slots, low))
    up_low, down_low = along(low, "blk", 1), along(low, "blk", -1)

    product = neighbour_product(current, hessian, slots)
    from_low, from_top, product = lax.optimization_barrier((up_low, down_top, product))
    far = [along(from_low, "blk", 1), along(from_top, "blk", -1)]
    pieces = first_sums(place, [low, top, down_low, down_top, up_low, up_top], product)
    pieces = lax.all_to_all(pieces, "dom", 0, 0, tiled=True)
    total, *far = lax.optimization_barrier((jnp.sum(pieces, axis=0), *far))
    stored = ordered(place, [low, top, down_low, down_top, *far, up_low, up_top])
    spread = lax.all_to_all(
        jnp.broadcast_to(total[None], pieces.shape), "dom", 0, 0, tiled=True
    )
    spread = over_blk(spread[: N_DOM // 2], spread[N_DOM // 2 : TILES])
    first, upper, inner = first_block(place, spread, product, stored, scale)

    product = neighbour_product(first, hessian, slots)
    kept, sent = second_sums(place, product, first, stored)
    part = kept + flipped(sent, 1)
    part = summed(part, unit_x, (1, 2, 3))
    part = summed(part, unit_z, (1,))
    part = summed(part, unit_z, (2, 4, 6))
    mine = [part] + [along(part, "blk", -k) for k in (1, 2, 3)]
    others = flipped(jnp.stack(mine), 1)
    return second_block(place, mine, others, inner, product, stored, first, upper, scale)


def solution(mesh):
    placed = (P("dom", None, None, None), P("dom", None), P("dom"), P("blk", "dom"))
    return jax.shard_map(
        local, mesh=mesh, in_specs=placed, out_specs=(P(None, "blk", "dom"), P()), check_vma=False
    )
```

```python
import functools

import jax
import jax.numpy as jnp
from jax import lax
from jax.experimental import pallas as pl
from jax.experimental.pallas import tpu as pltpu
from jax.sharding import PartitionSpec as P

BLOCK = 64
STORED = 512
N_DOM = 64
N_X, N_Z, N_CORE = 4, 8, 2
N_BLK = 4
OWN = BLOCK // N_BLK
TILES = 57
SPAN = 5
FETCH_LIMIT = 40
PRODUCT_LIMIT = 20


bf16 = jnp.bfloat16
f32 = jnp.float32


def split(value):
    top = value.astype(bf16)
    return top, (value - top.astype(f32)).astype(bf16)


def nt(a, b):
    rows = a.shape[0]
    dims = (((1,), (1,)), ((), ()))
    parts = jnp.concatenate(split(a), axis=0)
    b_top, b_rest = split(b)
    one = lax.dot_general(parts, b_top, dims, preferred_element_type=f32)
    two = lax.dot_general(parts, b_rest, dims, preferred_element_type=f32)
    return one[:rows] + (one[rows:] + two[:rows] + two[rows:])


def exactly(a, b, side):
    return lax.dot_general(
        a,
        b,
        (((1,), (side,)), ((), ())),
        precision=lax.Precision.HIGHEST,
        preferred_element_type=f32,
    )


def closely(a, b):
    rows = a.shape[0]
    dims = (((1,), (0,)), ((), ()))
    a_top, a_mid = split(a)
    a_low = (a - a_top.astype(f32) - a_mid.astype(f32)).astype(bf16)
    b_top, b_mid = split(b)
    b_low = (b - b_top.astype(f32) - b_mid.astype(f32)).astype(bf16)
    parts = jnp.concatenate([a_top, a_mid, a_low], axis=0)
    one = lax.dot_general(parts, b_top, dims, preferred_element_type=f32)
    two = lax.dot_general(parts[: 2 * rows], b_mid, dims, preferred_element_type=f32)
    three = lax.dot_general(a_top, b_low, dims, preferred_element_type=f32)
    small = one[2 * rows :] + two[rows:] + three
    return one[:rows] + (one[rows : 2 * rows] + two[:rows] + small)


def flipped(value, mask):
    return lax.ppermute(value, "dom", [(i, i ^ mask) for i in range(N_DOM)])


def along(value, axis, by):
    peers = lax.axis_size(axis)
    return lax.ppermute(value, axis, [(i, (i + by) % peers) for i in range(peers)])


def tree_sum(parts):
    while len(parts) > 1:
        parts = [parts[i] + parts[i + 1] for i in range(0, len(parts), 2)]
    return parts[0]


def summed(value, unit, steps):
    return tree_sum([value] + [flipped(value, unit * k) for k in steps])


VMEM = pl.BlockSpec(memory_space=pltpu.VMEM)
SMEM = pl.BlockSpec(memory_space=pltpu.SMEM)


def over_blk(low, top):
    up_low, down_top = along(low, "blk", 1), along(top, "blk", -1)
    up_top, down_low = along(top, "blk", 1), along(low, "blk", -1)
    far_low, far_top = along(up_low, "blk", 1), along(down_top, "blk", -1)
    return [low, top, down_low, down_top, far_low, far_top, up_low, up_top]


def fetch_kernel(hess_ref, after_ref, out_ref, sems):
    tiles = hess_ref.shape[0]
    copies = [pltpu.make_async_copy(hess_ref.at[t], out_ref.at[t], sems.at[t]) for t in range(tiles)]
    for copy in copies:
        copy.start()
    for copy in copies:
        copy.wait()


def fetched(hessian, after):
    return pl.pallas_call(
        fetch_kernel,
        out_shape=pltpu.VMEM(hessian.shape, f32),
        in_specs=[pl.BlockSpec(memory_space=pltpu.HBM), SMEM if after.dtype == jnp.int32 else VMEM],
        out_specs=VMEM,
        scratch_shapes=[pltpu.SemaphoreType.DMA((hessian.shape[0],))],
        compiler_params=pltpu.CompilerParams(vmem_limit_bytes=FETCH_LIMIT << 20),
        cost_estimate=pl.CostEstimate(flops=0, bytes_accessed=20 << 20, transcendentals=0),
        name="fetch",
    )(hessian, after)


def product_kernel(slots_ref, hess_ref, *refs):
    pieces, out_ref, parts, result = refs[:SPAN], *refs[SPAN:]
    tiles, listed, rows = hess_ref.shape[:3]
    for p in range(SPAN):
        values = pieces[p][...]
        for q in range(tiles):
            parts[tiles * p + q] = jnp.concatenate(
                split(values[:, rows * q : rows * (q + 1)]), axis=0
            )
    parts[SPAN * tiles] = jnp.zeros((2 * BLOCK, rows), bf16)
    dims = (((1,), (1,)), ((), ()))

    def tile(t, carry):
        first = jnp.zeros((2 * BLOCK, rows), f32)
        second = jnp.zeros((BLOCK, rows), f32)
        for k in range(listed):
            x = parts[slots_ref[t * listed + k]]
            top, rest = split(hess_ref[t, k])
            first = first + lax.dot_general(x, top, dims, preferred_element_type=f32)
            second = second + lax.dot_general(x[:BLOCK], rest, dims, preferred_element_type=f32)
        result[t] = first[:BLOCK] + (first[BLOCK:] + second)
        return carry

    lax.fori_loop(0, tiles, tile, 0)
    out_ref[...] = jnp.concatenate([result[t] for t in range(tiles)], axis=1)


def neighbour_product(block, held, slots):
    tiles, rows = held.shape[0], held.shape[2]
    pieces = [block] + [along(block, "dom", offset) for offset in (1, -1, 2, -2)]
    return pl.pallas_call(
        product_kernel,
        out_shape=jax.ShapeDtypeStruct(block.shape, f32),
        grid_spec=pltpu.PrefetchScalarGridSpec(
            num_scalar_prefetch=1,
            grid=(),
            in_specs=[VMEM] * (1 + SPAN),
            out_specs=VMEM,
            scratch_shapes=[
                pltpu.VMEM((SPAN * tiles + 1, 2 * BLOCK, rows), bf16),
                pltpu.VMEM((tiles, BLOCK, rows), f32),
            ],
        ),
        compiler_params=pltpu.CompilerParams(vmem_limit_bytes=PRODUCT_LIMIT << 20),
        cost_estimate=pl.CostEstimate(flops=4 << 30, bytes_accessed=12 << 20, transcendentals=0),
        name="neighbour_product",
    )(slots, held, *pieces)


def eliminated(gram):
    groups = BLOCK // 8
    lanes = 2 * BLOCK
    row_ids = lax.broadcasted_iota(jnp.int32, (8, lanes), 0)
    lane_ids = lax.broadcasted_iota(jnp.int32, (8, lanes), 1)
    wide = jnp.concatenate([gram, jnp.zeros((BLOCK, BLOCK), f32)], axis=1)
    a = [
        wide[8 * g : 8 * g + 8, :] + jnp.where(lane_ids == row_ids + (8 * g + BLOCK), 1.0, 0.0)
        for g in range(groups)
    ]
    pivots = []
    for p in range(groups):
        cols = [
            [jnp.broadcast_to(a[g][:, 8 * p + c : 8 * p + c + 1], (8, lanes)) for g in range(p, groups)]
            for c in range(8)
        ]
        kept = jnp.zeros((8, lanes), f32)
        for c in range(8):
            pivot = jnp.broadcast_to(cols[c][0][c : c + 1, :], (8, lanes))
            kept = jnp.where(row_ids == c, pivot, kept)
            inverse = 1.0 / pivot
            row = jnp.broadcast_to(a[p][c : c + 1, :], (8, lanes))
            scale = [f * inverse for f in cols[c]]
            scale[0] = jnp.where(row_ids > c, scale[0], 0.0)
            for g in range(p, groups):
                a[g] = a[g] - scale[g - p] * row
            for later in range(c + 1, 8):
                level = jnp.broadcast_to(cols[later][0][c : c + 1, :], (8, lanes))
                cols[later] = [u - s * level for u, s in zip(cols[later], scale)]
        pivots.append(kept)
    return [
        jnp.where(lane_ids < row_ids + 8 * g, 0.0, a[g] * lax.rsqrt(pivots[g]))
        for g in range(groups)
    ]


def chosen_kernel(place_ref, *refs):
    for k in range(N_BLK):

        @pl.when(place_ref[0] == k)
        def _(k=k):
            refs[N_BLK][...] = refs[k][...]


def chosen(place, options):
    return pl.pallas_call(
        chosen_kernel,
        out_shape=jax.ShapeDtypeStruct(options[0].shape, f32),
        in_specs=[SMEM] + [VMEM] * N_BLK,
        out_specs=VMEM,
        compiler_params=pltpu.CompilerParams(vmem_limit_bytes=8 << 20),
        cost_estimate=pl.CostEstimate(flops=0, bytes_accessed=1 << 19, transcendentals=0),
        name="chosen",
    )(place, *options)


def first_sums_kernel(place_ref, *refs):
    mine, after, before = [
        jnp.concatenate([refs[2 * k][...], refs[2 * k + 1][...]], axis=0) for k in range(3)
    ]
    product_ref, out_ref = refs[6], refs[7]
    for o, (a, b) in enumerate(((mine, mine), (mine, after), (before, after))):
        g = nt(a, b)
        for r in range(16):
            out_ref[16 * o + r] = g[8 * r : 8 * r + 8, :]
    c = nt(product_ref[...], mine)
    for h in range(8):
        out_ref[48 + h] = c[8 * h : 8 * h + 8, :]
    own = product_ref[pl.ds(pl.multiple_of(place_ref[0] * OWN, OWN), OWN), :]
    squares = nt(own, product_ref[...])
    out_ref[56] = jnp.concatenate([squares[:8], squares[8:]], axis=1)
    for q in range(TILES, N_DOM):
        out_ref[q] = jnp.zeros((8, 128), f32)


def first_sums(place, pieces, product):
    return pl.pallas_call(
        first_sums_kernel,
        out_shape=jax.ShapeDtypeStruct((N_DOM, 8, 128), f32),
        in_specs=[SMEM] + [VMEM] * 7,
        out_specs=VMEM,
        compiler_params=pltpu.CompilerParams(vmem_limit_bytes=20 << 20),
        cost_estimate=pl.CostEstimate(flops=2 << 30, bytes_accessed=4 << 20, transcendentals=0),
        name="first_sums",
    )(place, *pieces, product)


def ordered_kernel(place_ref, *refs):
    for k in range(8):
        row = ((place_ref[0] + k // 2) % N_BLK * 2 + k % 2) * BLOCK
        refs[8][pl.ds(pl.multiple_of(row, BLOCK), BLOCK), :] = refs[k][...]


def ordered(place, pieces):
    return pl.pallas_call(
        ordered_kernel,
        out_shape=jax.ShapeDtypeStruct((STORED, pieces[0].shape[1]), f32),
        in_specs=[SMEM] + [VMEM] * 8,
        out_specs=VMEM,
        compiler_params=pltpu.CompilerParams(vmem_limit_bytes=16 << 20),
        cost_estimate=pl.CostEstimate(flops=0, bytes_accessed=3 << 20, transcendentals=0),
        name="ordered",
    )(place, *pieces)


def finished(c, squares, inner, product, stored, fresh=None):
    d = 2.0 * c - exactly(c, inner, 0)
    f = c - exactly(d, inner, 0)
    both = jnp.concatenate(eliminated(squares - exactly(c, d, 1) - exactly(d, f, 1)), axis=0)
    upper, inverse = both[:, :BLOCK], both[:, BLOCK:]
    if fresh is not None:
        product = product - closely(d[:, :BLOCK], fresh)
        d = jnp.where(lax.broadcasted_iota(jnp.int32, d.shape, 1) < BLOCK, 0.0, d)
    return closely(inverse, product - closely(d, stored)), upper, exactly(inverse, f, 0)


def first_block_kernel(scale, place_ref, *refs):
    pieces, product_ref, stored_ref = refs[:8], refs[8], refs[9]
    block_ref, upper_ref, inner_ref, held = refs[10:]
    me = place_ref[0]
    for k in range(8):
        held[((me + k // 2) % N_BLK) * 2 + k % 2, : pieces[k].shape[0]] = pieces[k][...] * scale
    for b in range(N_BLK):
        for o, (i, j) in enumerate(((b, b), (b, b + 1), (b - 1, b + 1))):
            i, j = 128 * (i % N_BLK), 128 * (j % N_BLK)
            g = [held[2 * b + (16 * o + r) // 32, (16 * o + r) % 32] for r in range(16)]
            g = jnp.concatenate(g, axis=0)
            inner_ref[i : i + 128, j : j + 128] = g
            if o == 1:
                inner_ref[j : j + 128, i : i + 128] = g.T
    c = jnp.concatenate(
        [
            jnp.concatenate([held[2 * b + 1, 16 + h] for b in range(N_BLK)], axis=1)
            for h in range(8)
        ],
        axis=0,
    )
    squares = [held[2 * i + 1, 24] for i in range(N_BLK)]
    squares = jnp.concatenate([s[:, BLOCK * h : BLOCK * h + BLOCK] for s in squares for h in range(2)], axis=0)
    block_ref[...], upper_ref[...], crossed = finished(
        c, squares, inner_ref[...], product_ref[...], stored_ref[...]
    )
    rows = lax.broadcasted_iota(jnp.int32, crossed.shape, 0)
    lanes = lax.broadcasted_iota(jnp.int32, crossed.shape, 1)
    inner_ref[:BLOCK, :] = jnp.where(lanes < BLOCK, jnp.where(lanes == rows, 1.0, 0.0), crossed)
    inner_ref[BLOCK:, :BLOCK] = crossed.T[BLOCK:]


def first_block(place, pieces, product, stored, scale):
    shapes = [product.shape, (BLOCK, BLOCK), (STORED, STORED)]
    return pl.pallas_call(
        functools.partial(first_block_kernel, scale),
        out_shape=[jax.ShapeDtypeStruct(s, f32) for s in shapes],
        in_specs=[SMEM] + [VMEM] * 10,
        out_specs=[VMEM] * 3,
        scratch_shapes=[pltpu.VMEM((2 * N_BLK, N_DOM // 2, 8, 128), f32)],
        compiler_params=pltpu.CompilerParams(vmem_limit_bytes=24 << 20),
        cost_estimate=pl.CostEstimate(flops=2 << 30, bytes_accessed=6 << 20, transcendentals=0),
        name="first_block",
    )(place, *pieces, product, stored)


def second_sums_kernel(place_ref, product_ref, fresh_ref, stored_ref, kept_ref, sent_ref, sums):
    me, core = place_ref[0], place_ref[1]
    own = product_ref[pl.ds(pl.multiple_of(me * OWN, OWN), OWN), :]
    sums[:, :STORED] = nt(own, stored_ref[...])
    sums[:, :BLOCK] = nt(own, fresh_ref[...])
    sums[:, STORED:] = nt(own, product_ref[...])
    half = OWN // N_CORE
    kept_ref[...] = sums[pl.ds(pl.multiple_of(core * half, half), half), :]
    sent_ref[...] = sums[pl.ds(pl.multiple_of((1 - core) * half, half), half), :]


def second_sums(place, product, fresh, stored):
    return pl.pallas_call(
        second_sums_kernel,
        out_shape=[jax.ShapeDtypeStruct((OWN // N_CORE, STORED + BLOCK), f32)] * 2,
        in_specs=[SMEM] + [VMEM] * 3,
        out_specs=[VMEM] * 2,
        scratch_shapes=[pltpu.VMEM((OWN, STORED + BLOCK), f32)],
        compiler_params=pltpu.CompilerParams(vmem_limit_bytes=16 << 20),
        cost_estimate=pl.CostEstimate(flops=1 << 28, bytes_accessed=2 << 20, transcendentals=0),
        name="second_sums",
    )(place, product, fresh, stored)


def second_block_kernel(scale, place_ref, *refs):
    mine, others = refs[:4], refs[4]
    inner_ref, product_ref, stored_ref, fresh_ref, upper_ref = refs[5:10]
    blocks_ref, factors_ref, sums, whole = refs[10:]
    me, core = place_ref[0], place_ref[1]
    for k in range(N_BLK):
        row = (me + k) % N_BLK * OWN
        sums[pl.ds(pl.multiple_of(row + core * 8, 8), 8), :] = mine[k][...] * scale
        sums[pl.ds(pl.multiple_of(row + (1 - core) * 8, 8), 8), :] = others[k] * scale
    block, factors_ref[1], _ = finished(
        sums[:, :STORED],
        sums[:, STORED:],
        inner_ref[...],
        product_ref[...],
        stored_ref[...],
        fresh_ref[...],
    )
    whole[...] = block
    rows = pl.ds(pl.multiple_of(me * OWN, OWN), OWN)
    blocks_ref[0] = fresh_ref[rows, :]
    blocks_ref[1] = whole[rows, :]
    factors_ref[0] = upper_ref[...]


def second_block(place, mine, others, inner, product, stored, fresh, upper, scale):
    return pl.pallas_call(
        functools.partial(second_block_kernel, scale),
        out_shape=[
            jax.ShapeDtypeStruct((2, OWN, product.shape[1]), f32),
            jax.ShapeDtypeStruct((2, BLOCK, BLOCK), f32),
        ],
        in_specs=[SMEM] + [VMEM] * 10,
        out_specs=[VMEM] * 2,
        scratch_shapes=[
            pltpu.VMEM((BLOCK, STORED + BLOCK), f32),
            pltpu.VMEM(product.shape, f32),
        ],
        compiler_params=pltpu.CompilerParams(vmem_limit_bytes=24 << 20),
        cost_estimate=pl.CostEstimate(flops=2 << 30, bytes_accessed=6 << 20, transcendentals=0),
        name="second_block",
    )(place, *mine, others, inner, product, stored, fresh, upper)


def local(hessian, neighbours, counts, basis_vectors):
    me = lax.axis_index("blk")
    dom = lax.axis_index("dom")
    place = jnp.stack([me, dom % N_CORE]).astype(jnp.int32)
    unit_z, unit_x = N_CORE, N_CORE * N_Z
    tiles, listed = neighbours.shape
    scale = 1.0 / (basis_vectors.shape[1] * N_DOM)

    slots = (neighbours // tiles - dom + 2) % N_DOM
    slots = jnp.where(
        slots < 2, 3 - 2 * slots, jnp.where(slots == 2, 0, jnp.where(slots == 3, 2, 4))
    )
    slots = slots * tiles + neighbours % tiles
    live = jnp.arange(listed)[None, :] < counts[:, None]
    slots = jnp.where(live, slots, SPAN * tiles).reshape(-1)

    low, top = lax.optimization_barrier((basis_vectors[:BLOCK], basis_vectors[BLOCK:]))
    up_top, down_top = along(top, "blk", 1), along(top, "blk", -1)
    across = lax.ppermute(top, "blk", [(3, 1)])
    top, slots, place = lax.optimization_barrier((top, slots, place))
    held = fetched(hessian, place)
    up_top, across, down_top, slots, held = lax.optimization_barrier(
        (up_top, across, down_top, slots, held)
    )
    current = chosen(place, [up_top, across, down_top, top])
    current, slots, low = lax.optimization_barrier((current, slots, low))
    up_low, down_low = along(low, "blk", 1), along(low, "blk", -1)

    product = neighbour_product(current, held, slots)
    from_low, from_top, product = lax.optimization_barrier((up_low, down_top, product))
    far = [along(from_low, "blk", 1), along(from_top, "blk", -1)]
    pieces = first_sums(place, [low, top, down_low, down_top, up_low, up_top], product)
    pieces = lax.all_to_all(pieces, "dom", 0, 0, tiled=True)
    total, *far = lax.optimization_barrier((jnp.sum(pieces, axis=0), *far))
    stored = ordered(place, [low, top, down_low, down_top, *far, up_low, up_top])
    spread = lax.all_to_all(
        jnp.broadcast_to(total[None], pieces.shape), "dom", 0, 0, tiled=True
    )
    spread = over_blk(spread[: N_DOM // 2], spread[N_DOM // 2 : TILES])
    held = fetched(hessian, spread[0])
    *spread, held = lax.optimization_barrier((*spread, held))
    first, upper, inner = first_block(place, spread, product, stored, scale)

    product = neighbour_product(first, held, slots)
    kept, sent = second_sums(place, product, first, stored)
    part = kept + flipped(sent, 1)
    part = summed(part, unit_x, (1, 2, 3))
    part = summed(part, unit_z, (1,))
    part = summed(part, unit_z, (2, 4, 6))
    mine = [part] + [along(part, "blk", -k) for k in (1, 2, 3)]
    others = flipped(jnp.stack(mine), 1)
    return second_block(place, mine, others, inner, product, stored, first, upper, scale)


def solution(mesh):
    placed = (P("dom", None, None, None), P("dom", None), P("dom"), P("blk", "dom"))
    return jax.shard_map(
        local, mesh=mesh, in_specs=placed, out_specs=(P(None, "blk", "dom"), P()), check_vma=False
    )
```

```python
import functools

import jax
import jax.numpy as jnp
from jax import lax
from jax.experimental import pallas as pl
from jax.experimental.pallas import tpu as pltpu
from jax.sharding import PartitionSpec as P

BLOCK = 64
STORED = 512
N_DOM = 64
N_X, N_Z, N_CORE = 4, 8, 2
N_BLK = 4
OWN = BLOCK // N_BLK
TILES = 57
SPAN = 5
FETCH_LIMIT = 40
PRODUCT_LIMIT = 20


bf16 = jnp.bfloat16
f32 = jnp.float32


def split(value):
    top = value.astype(bf16)
    return top, (value - top.astype(f32)).astype(bf16)


def product_of(a, b, side):
    rows = a.shape[0]
    dims = (((1,), (side,)), ((), ()))
    parts = jnp.concatenate(split(a), axis=0)
    b_top, b_rest = split(b)
    one = lax.dot_general(parts, b_top, dims, preferred_element_type=f32)
    two = lax.dot_general(parts, b_rest, dims, preferred_element_type=f32)
    return one[:rows] + (one[rows:] + two[:rows] + two[rows:])


def nt(a, b):
    return product_of(a, b, 1)


def nn(a, b):
    return product_of(a, b, 0)


def flipped(value, mask):
    return lax.ppermute(value, "dom", [(i, i ^ mask) for i in range(N_DOM)])


def along(value, axis, by):
    peers = lax.axis_size(axis)
    return lax.ppermute(value, axis, [(i, (i + by) % peers) for i in range(peers)])


def tree_sum(parts):
    while len(parts) > 1:
        parts = [parts[i] + parts[i + 1] for i in range(0, len(parts), 2)]
    return parts[0]


def summed(value, unit, steps):
    return tree_sum([value] + [flipped(value, unit * k) for k in steps])


VMEM = pl.BlockSpec(memory_space=pltpu.VMEM)
SMEM = pl.BlockSpec(memory_space=pltpu.SMEM)


def over_blk(low, top):
    up_low, down_top = along(low, "blk", 1), along(top, "blk", -1)
    up_top, down_low = along(top, "blk", 1), along(low, "blk", -1)
    far_low, far_top = along(up_low, "blk", 1), along(down_top, "blk", -1)
    return [low, top, down_low, down_top, far_low, far_top, up_low, up_top]


def fetch_kernel(hess_ref, after_ref, out_ref, sems):
    tiles = hess_ref.shape[0]
    copies = [pltpu.make_async_copy(hess_ref.at[t], out_ref.at[t], sems.at[t]) for t in range(tiles)]
    for copy in copies:
        copy.start()
    for copy in copies:
        copy.wait()


def fetched(hessian, after):
    return pl.pallas_call(
        fetch_kernel,
        out_shape=pltpu.VMEM(hessian.shape, f32),
        in_specs=[pl.BlockSpec(memory_space=pltpu.HBM), VMEM],
        out_specs=VMEM,
        scratch_shapes=[pltpu.SemaphoreType.DMA((hessian.shape[0],))],
        compiler_params=pltpu.CompilerParams(vmem_limit_bytes=FETCH_LIMIT << 20),
        cost_estimate=pl.CostEstimate(flops=0, bytes_accessed=20 << 20, transcendentals=0),
        name="fetch",
    )(hessian, after)


def product_kernel(slots_ref, hess_ref, *refs):
    pieces, out_ref, parts, result = refs[:SPAN], *refs[SPAN:]
    tiles, listed, rows = hess_ref.shape[:3]
    for p in range(SPAN):
        values = pieces[p][...]
        for q in range(tiles):
            parts[tiles * p + q] = jnp.concatenate(
                split(values[:, rows * q : rows * (q + 1)]), axis=0
            )
    parts[SPAN * tiles] = jnp.zeros((2 * BLOCK, rows), bf16)
    dims = (((1,), (1,)), ((), ()))

    def tile(t, carry):
        first = jnp.zeros((2 * BLOCK, rows), f32)
        second = jnp.zeros((BLOCK, rows), f32)
        for k in range(listed):
            x = parts[slots_ref[t * listed + k]]
            top, rest = split(hess_ref[t, k])
            first = first + lax.dot_general(x, top, dims, preferred_element_type=f32)
            second = second + lax.dot_general(x[:BLOCK], rest, dims, preferred_element_type=f32)
        result[t] = first[:BLOCK] + (first[BLOCK:] + second)
        return carry

    lax.fori_loop(0, tiles, tile, 0)
    out_ref[...] = jnp.concatenate([result[t] for t in range(tiles)], axis=1)


def neighbour_product(block, hessian, slots):
    tiles, rows = hessian.shape[0], hessian.shape[2]
    pieces = [block] + [along(block, "dom", offset) for offset in (1, -1, 2, -2)]
    held = fetched(hessian, block)
    return pl.pallas_call(
        product_kernel,
        out_shape=jax.ShapeDtypeStruct(block.shape, f32),
        grid_spec=pltpu.PrefetchScalarGridSpec(
            num_scalar_prefetch=1,
            grid=(),
            in_specs=[VMEM] * (1 + SPAN),
            out_specs=VMEM,
            scratch_shapes=[
                pltpu.VMEM((SPAN * tiles + 1, 2 * BLOCK, rows), bf16),
                pltpu.VMEM((tiles, BLOCK, rows), f32),
            ],
        ),
        compiler_params=pltpu.CompilerParams(vmem_limit_bytes=PRODUCT_LIMIT << 20),
        cost_estimate=pl.CostEstimate(flops=4 << 30, bytes_accessed=12 << 20, transcendentals=0),
        name="neighbour_product",
    )(slots, held, *pieces)


def eliminated(gram):
    groups = BLOCK // 8
    lanes = 2 * BLOCK
    row_ids = lax.broadcasted_iota(jnp.int32, (8, lanes), 0)
    lane_ids = lax.broadcasted_iota(jnp.int32, (8, lanes), 1)
    wide = jnp.concatenate([gram, jnp.zeros((BLOCK, BLOCK), f32)], axis=1)
    a = [
        wide[8 * g : 8 * g + 8, :] + jnp.where(lane_ids == row_ids + (8 * g + BLOCK), 1.0, 0.0)
        for g in range(groups)
    ]
    pivots = []
    for p in range(groups):
        cols = [
            [jnp.broadcast_to(a[g][:, 8 * p + c : 8 * p + c + 1], (8, lanes)) for g in range(p, groups)]
            for c in range(8)
        ]
        kept = jnp.zeros((8, lanes), f32)
        for c in range(8):
            pivot = jnp.broadcast_to(cols[c][0][c : c + 1, :], (8, lanes))
            kept = jnp.where(row_ids == c, pivot, kept)
            inverse = 1.0 / pivot
            row = jnp.broadcast_to(a[p][c : c + 1, :], (8, lanes))
            scale = [f * inverse for f in cols[c]]
            scale[0] = jnp.where(row_ids > c, scale[0], 0.0)
            for g in range(p, groups):
                a[g] = a[g] - scale[g - p] * row
            for later in range(c + 1, 8):
                level = jnp.broadcast_to(cols[later][0][c : c + 1, :], (8, lanes))
                cols[later] = [u - s * level for u, s in zip(cols[later], scale)]
        pivots.append(kept)
    return [
        jnp.where(lane_ids < row_ids + 8 * g, 0.0, a[g] * lax.rsqrt(pivots[g]))
        for g in range(groups)
    ]


def chosen_kernel(place_ref, *refs):
    for k in range(N_BLK):

        @pl.when(place_ref[0] == k)
        def _(k=k):
            refs[N_BLK][...] = refs[k][...]


def chosen(place, options):
    return pl.pallas_call(
        chosen_kernel,
        out_shape=jax.ShapeDtypeStruct(options[0].shape, f32),
        in_specs=[SMEM] + [VMEM] * N_BLK,
        out_specs=VMEM,
        compiler_params=pltpu.CompilerParams(vmem_limit_bytes=8 << 20),
        cost_estimate=pl.CostEstimate(flops=0, bytes_accessed=1 << 19, transcendentals=0),
        name="chosen",
    )(place, *options)


def first_sums_kernel(place_ref, *refs):
    mine, after, before = [
        jnp.concatenate([refs[2 * k][...], refs[2 * k + 1][...]], axis=0) for k in range(3)
    ]
    product_ref, out_ref = refs[6], refs[7]
    for o, (a, b) in enumerate(((mine, mine), (mine, after), (before, after))):
        g = nt(a, b)
        for r in range(16):
            out_ref[16 * o + r] = g[8 * r : 8 * r + 8, :]
    c = nt(product_ref[...], mine)
    for h in range(8):
        out_ref[48 + h] = c[8 * h : 8 * h + 8, :]
    own = product_ref[pl.ds(pl.multiple_of(place_ref[0] * OWN, OWN), OWN), :]
    squares = nt(own, product_ref[...])
    out_ref[56] = jnp.concatenate([squares[:8], squares[8:]], axis=1)
    for q in range(TILES, N_DOM):
        out_ref[q] = jnp.zeros((8, 128), f32)


def first_sums(place, pieces, product):
    return pl.pallas_call(
        first_sums_kernel,
        out_shape=jax.ShapeDtypeStruct((N_DOM, 8, 128), f32),
        in_specs=[SMEM] + [VMEM] * 7,
        out_specs=VMEM,
        compiler_params=pltpu.CompilerParams(vmem_limit_bytes=20 << 20),
        cost_estimate=pl.CostEstimate(flops=2 << 30, bytes_accessed=4 << 20, transcendentals=0),
        name="first_sums",
    )(place, *pieces, product)


def ordered_kernel(place_ref, *refs):
    for k in range(8):
        row = ((place_ref[0] + k // 2) % N_BLK * 2 + k % 2) * BLOCK
        refs[8][pl.ds(pl.multiple_of(row, BLOCK), BLOCK), :] = refs[k][...]


def ordered(place, pieces):
    return pl.pallas_call(
        ordered_kernel,
        out_shape=jax.ShapeDtypeStruct((STORED, pieces[0].shape[1]), f32),
        in_specs=[SMEM] + [VMEM] * 8,
        out_specs=VMEM,
        compiler_params=pltpu.CompilerParams(vmem_limit_bytes=16 << 20),
        cost_estimate=pl.CostEstimate(flops=0, bytes_accessed=3 << 20, transcendentals=0),
        name="ordered",
    )(place, *pieces)


def finished(c, squares, inner, product, stored, fresh=None):
    d = 2.0 * c - nn(c, inner)
    f = c - nn(d, inner)
    both = jnp.concatenate(eliminated(squares - nt(c, d) - nt(d, f)), axis=0)
    upper, inverse = both[:, :BLOCK], both[:, BLOCK:]
    if fresh is not None:
        product = product - nn(d[:, :BLOCK], fresh)
        d = jnp.where(lax.broadcasted_iota(jnp.int32, d.shape, 1) < BLOCK, 0.0, d)
    return nn(inverse, product - nn(d, stored)), upper, nn(inverse, f)


def first_block_kernel(scale, place_ref, *refs):
    pieces, product_ref, stored_ref = refs[:8], refs[8], refs[9]
    block_ref, upper_ref, inner_ref, held = refs[10:]
    me = place_ref[0]
    for k in range(8):
        held[((me + k // 2) % N_BLK) * 2 + k % 2, : pieces[k].shape[0]] = pieces[k][...] * scale
    for b in range(N_BLK):
        for o, (i, j) in enumerate(((b, b), (b, b + 1), (b - 1, b + 1))):
            i, j = 128 * (i % N_BLK), 128 * (j % N_BLK)
            g = [held[2 * b + (16 * o + r) // 32, (16 * o + r) % 32] for r in range(16)]
            g = jnp.concatenate(g, axis=0)
            inner_ref[i : i + 128, j : j + 128] = g
            if o == 1:
                inner_ref[j : j + 128, i : i + 128] = g.T
    c = jnp.concatenate(
        [
            jnp.concatenate([held[2 * b + 1, 16 + h] for b in range(N_BLK)], axis=1)
            for h in range(8)
        ],
        axis=0,
    )
    squares = [held[2 * i + 1, 24] for i in range(N_BLK)]
    squares = jnp.concatenate([s[:, BLOCK * h : BLOCK * h + BLOCK] for s in squares for h in range(2)], axis=0)
    block_ref[...], upper_ref[...], crossed = finished(
        c, squares, inner_ref[...], product_ref[...], stored_ref[...]
    )
    rows = lax.broadcasted_iota(jnp.int32, crossed.shape, 0)
    lanes = lax.broadcasted_iota(jnp.int32, crossed.shape, 1)
    inner_ref[:BLOCK, :] = jnp.where(lanes < BLOCK, jnp.where(lanes == rows, 1.0, 0.0), crossed)
    inner_ref[BLOCK:, :BLOCK] = crossed.T[BLOCK:]


def first_block(place, pieces, product, stored, scale):
    shapes = [product.shape, (BLOCK, BLOCK), (STORED, STORED)]
    return pl.pallas_call(
        functools.partial(first_block_kernel, scale),
        out_shape=[jax.ShapeDtypeStruct(s, f32) for s in shapes],
        in_specs=[SMEM] + [VMEM] * 10,
        out_specs=[VMEM] * 3,
        scratch_shapes=[pltpu.VMEM((2 * N_BLK, N_DOM // 2, 8, 128), f32)],
        compiler_params=pltpu.CompilerParams(vmem_limit_bytes=24 << 20),
        cost_estimate=pl.CostEstimate(flops=2 << 30, bytes_accessed=6 << 20, transcendentals=0),
        name="first_block",
    )(place, *pieces, product, stored)


def second_sums_kernel(place_ref, product_ref, fresh_ref, stored_ref, kept_ref, sent_ref, sums):
    me, core = place_ref[0], place_ref[1]
    own = product_ref[pl.ds(pl.multiple_of(me * OWN, OWN), OWN), :]
    sums[:, :STORED] = nt(own, stored_ref[...])
    sums[:, :BLOCK] = nt(own, fresh_ref[...])
    sums[:, STORED:] = nt(own, product_ref[...])
    half = OWN // N_CORE
    kept_ref[...] = sums[pl.ds(pl.multiple_of(core * half, half), half), :]
    sent_ref[...] = sums[pl.ds(pl.multiple_of((1 - core) * half, half), half), :]


def second_sums(place, product, fresh, stored):
    return pl.pallas_call(
        second_sums_kernel,
        out_shape=[jax.ShapeDtypeStruct((OWN // N_CORE, STORED + BLOCK), f32)] * 2,
        in_specs=[SMEM] + [VMEM] * 3,
        out_specs=[VMEM] * 2,
        scratch_shapes=[pltpu.VMEM((OWN, STORED + BLOCK), f32)],
        compiler_params=pltpu.CompilerParams(vmem_limit_bytes=16 << 20),
        cost_estimate=pl.CostEstimate(flops=1 << 28, bytes_accessed=2 << 20, transcendentals=0),
        name="second_sums",
    )(place, product, fresh, stored)


def second_block_kernel(scale, place_ref, *refs):
    mine, others = refs[:4], refs[4]
    inner_ref, product_ref, stored_ref, fresh_ref, upper_ref = refs[5:10]
    blocks_ref, factors_ref, sums, whole = refs[10:]
    me, core = place_ref[0], place_ref[1]
    for k in range(N_BLK):
        row = (me + k) % N_BLK * OWN
        sums[pl.ds(pl.multiple_of(row + core * 8, 8), 8), :] = mine[k][...] * scale
        sums[pl.ds(pl.multiple_of(row + (1 - core) * 8, 8), 8), :] = others[k] * scale
    block, factors_ref[1], _ = finished(
        sums[:, :STORED],
        sums[:, STORED:],
        inner_ref[...],
        product_ref[...],
        stored_ref[...],
        fresh_ref[...],
    )
    whole[...] = block
    rows = pl.ds(pl.multiple_of(me * OWN, OWN), OWN)
    blocks_ref[0] = fresh_ref[rows, :]
    blocks_ref[1] = whole[rows, :]
    factors_ref[0] = upper_ref[...]


def second_block(place, mine, others, inner, product, stored, fresh, upper, scale):
    return pl.pallas_call(
        functools.partial(second_block_kernel, scale),
        out_shape=[
            jax.ShapeDtypeStruct((2, OWN, product.shape[1]), f32),
            jax.ShapeDtypeStruct((2, BLOCK, BLOCK), f32),
        ],
        in_specs=[SMEM] + [VMEM] * 10,
        out_specs=[VMEM] * 2,
        scratch_shapes=[
            pltpu.VMEM((BLOCK, STORED + BLOCK), f32),
            pltpu.VMEM(product.shape, f32),
        ],
        compiler_params=pltpu.CompilerParams(vmem_limit_bytes=24 << 20),
        cost_estimate=pl.CostEstimate(flops=2 << 30, bytes_accessed=6 << 20, transcendentals=0),
        name="second_block",
    )(place, *mine, others, inner, product, stored, fresh, upper)


def local(hessian, neighbours, counts, basis_vectors):
    me = lax.axis_index("blk")
    dom = lax.axis_index("dom")
    place = jnp.stack([me, dom % N_CORE]).astype(jnp.int32)
    unit_z, unit_x = N_CORE, N_CORE * N_Z
    tiles, listed = neighbours.shape
    scale = 1.0 / (basis_vectors.shape[1] * N_DOM)

    slots = (neighbours // tiles - dom + 2) % N_DOM
    slots = jnp.where(
        slots < 2, 3 - 2 * slots, jnp.where(slots == 2, 0, jnp.where(slots == 3, 2, 4))
    )
    slots = slots * tiles + neighbours % tiles
    live = jnp.arange(listed)[None, :] < counts[:, None]
    slots = jnp.where(live, slots, SPAN * tiles).reshape(-1)

    low, top = lax.optimization_barrier((basis_vectors[:BLOCK], basis_vectors[BLOCK:]))
    up_top, down_top = along(top, "blk", 1), along(top, "blk", -1)
    across = lax.ppermute(top, "blk", [(3, 1)])
    current = chosen(place, [up_top, across, down_top, top])
    current, slots, low = lax.optimization_barrier((current, slots, low))
    up_low, down_low = along(low, "blk", 1), along(low, "blk", -1)

    product = neighbour_product(current, hessian, slots)
    from_low, from_top, product = lax.optimization_barrier((up_low, down_top, product))
    far = [along(from_low, "blk", 1), along(from_top, "blk", -1)]
    pieces = first_sums(place, [low, top, down_low, down_top, up_low, up_top], product)
    pieces = lax.all_to_all(pieces, "dom", 0, 0, tiled=True)
    total, *far = lax.optimization_barrier((jnp.sum(pieces, axis=0), *far))
    stored = ordered(place, [low, top, down_low, down_top, *far, up_low, up_top])
    spread = lax.all_to_all(
        jnp.broadcast_to(total[None], pieces.shape), "dom", 0, 0, tiled=True
    )
    spread = over_blk(spread[: N_DOM // 2], spread[N_DOM // 2 : TILES])
    first, upper, inner = first_block(place, spread, product, stored, scale)

    product = neighbour_product(first, hessian, slots)
    kept, sent = second_sums(place, product, first, stored)
    part = kept + flipped(sent, 1)
    part = summed(part, unit_x, (1, 2, 3))
    part = summed(part, unit_z, (1,))
    part = summed(part, unit_z, (2, 4, 6))
    mine = [part] + [along(part, "blk", -k) for k in (1, 2, 3)]
    others = flipped(jnp.stack(mine), 1)
    return second_block(place, mine, others, inner, product, stored, first, upper, scale)


def solution(mesh):
    placed = (P("dom", None, None, None), P("dom", None), P("dom"), P("blk", "dom"))
    return jax.shard_map(
        local, mesh=mesh, in_specs=placed, out_specs=(P(None, "blk", "dom"), P()), check_vma=False
    )
```
